256 devices in a mesh: chan: 4 (over x), mset: 8 (over y, core), blk: 8 (over z).
Axes of the slice: x: 4, y: 4, z: 8, core: 2. Of those that a mesh axis runs over, the one named last changes fastest.
Arguments:
- harmonics: bfloat16 [2, 3, 64, 1536], P(None, None, ('mset', 'blk'), 'chan'), may hold values from -6 to 6
- mixing: float32 [12, 3], replicated, may hold values from 0.2 to 1.2
- beam_window: float32 [12, 1536], P(None, 'chan'), may hold values from 0.2 to 1
- prior_inv: float32 [3, 1536], P(None, 'chan'), may hold values from 0.3 to 3
- legendre: bfloat16 [64, 1536, 8192], P(('mset', 'blk'), 'chan'), may hold values from -0.15625 to 0.15625
- inv_noise: bfloat16 [12, 8192, 8192], P('chan', ('mset', 'blk')), may hold values from 0.0099487305 to 0.099609375
- mode_index: int32 [64], replicated, may hold values from 0 to 1535, as said below
- cycle_pixels: int32 [12], replicated, may hold values from 2048 to 8192, as said below
Outputs:
- applied: float32 [2, 3, 64, 1536], P(None, None, ('mset', 'blk'), 'chan')
The draws below stay inside these ranges and needn't reach their ends.
Inputs may be any that keep to these rules, and one draw needn't show every extreme that they name: `mode_index`: distinct values; 0 and 1535 are always among them. `cycle_pixels`: each value is 2048, 4096 or 8192; every draw holds both the smallest and the largest.
All inputs are finite; a program needn't handle non-finite values.
Results may differ from the reference program's by a relative error of at most 0.005.
Values may be sent and summed in bfloat16 or wider, within the bound.
No kernel may reach another device: no remote copies, remote signals or barrier semaphores. Data moves between devices by JAX's collectives and lax.ppermute only.
A program may use at most 128 MiB of HBM per device.

```python
import math
import jax
import jax.numpy as jnp
from jax import lax

K = 3
L = 1536
PIX = 8192
NCH = 12
M = 64
R = 8192


def draw_mode_index(key, part):
    leading_key, second_key = jax.random.split(key)
    inner = jax.random.permutation(leading_key, L - 2)[:M - 2].astype(jnp.int32) + 1
    edges = jnp.array([0, L - 1], dtype=jnp.int32)
    whole = jnp.concatenate([edges, inner])
    return jax.random.permutation(second_key, whole).astype(jnp.int32)


def draw_cycle_pixels(key, part):
    leading_key, second_key = jax.random.split(key)
    levels = jax.random.randint(leading_key, (NCH,), 0, 3)
    values = jnp.where(levels == 0, PIX // 4, jnp.where(levels == 1, PIX // 2, PIX)).astype(jnp.int32)
    chosen = jax.random.permutation(second_key, NCH)
    values = values.at[chosen[0]].set(PIX)
    values = values.at[chosen[1]].set(PIX // 4)
    return values.astype(jnp.int32)


def block_levels(stream_key, extent, pieces, low, largest):
    def one(dim, blocks):
        heights = jax.random.uniform(jax.random.fold_in(jax.random.fold_in(stream_key, 6), dim), (blocks,), jnp.float32, low / len(pieces), largest / len(pieces))
        return jnp.repeat(jnp.exp(heights), extent[dim] // blocks).reshape((-1,) + (1,) * (len(extent) - dim - 1))

    loudness = one(*pieces[0])
    for cut in pieces[1:]:
        loudness = loudness * one(*cut)
    return loudness


def normal_values(rng, extent, spread, limit, shards=(), kind=jnp.bfloat16):
    values = jax.random.normal(rng, extent, jnp.float32) * spread
    if len(shards) > 0:
        values = block_levels(rng, extent, shards, -0.22, 0.18) * values
    return jnp.clip(values, min=-limit, max=limit).astype(kind)


def setup_inputs(seed: int = 0) -> dict:
    key_of = jax.random.split(jax.random.key(seed), 9)
    harmonics = normal_values(key_of[0], (2, K, M, L), 1.0, 6.0, ((2, 64), (3, 4)))
    mixing = jnp.clip(jax.random.uniform(key_of[1], (NCH, K), jnp.float32, 0.2, 1.2), 0.2, 1.2)
    beam_window = jnp.clip(jnp.exp(math.log(1.0) - 1.609438 * jax.random.uniform(key_of[2], (NCH, L), jnp.float32) ** block_levels(key_of[2], (NCH, L), ((1, 4),), -0.2, 0.2)), 0.2, 1.0)
    prior_inv = jnp.clip(jnp.exp(math.log(3.0) - 2.3025851 * jax.random.uniform(key_of[3], (K, L), jnp.float32) ** block_levels(key_of[3], (K, L), ((1, 4),), -0.2, 0.2)), 0.3, 3.0)
    legendre = normal_values(key_of[4], (M, L, R), L ** -0.5, 0.15625, ((0, 64), (1, 4)))
    inv_noise = jnp.clip(jnp.exp(math.log(0.099609375) - 2.3038113 * jax.random.uniform(key_of[5], (NCH, R, PIX), jnp.float32) ** block_levels(key_of[5], (NCH, R, PIX), ((0, 4), (1, 64)), -0.2, 0.2)), 0.0099487305, 0.099609375).astype(jnp.bfloat16)
    mode_index = draw_mode_index(jax.random.fold_in(key_of[8], 71), 0)
    cycle_pixels = draw_cycle_pixels(jax.random.fold_in(key_of[8], 71), 0)
    return dict(harmonics=harmonics, mixing=mixing, beam_window=beam_window, prior_inv=prior_inv, legendre=legendre, inv_noise=inv_noise, mode_index=mode_index, cycle_pixels=cycle_pixels)


def dft_table(mode_index, npix):
    pix_index = jnp.arange(PIX).astype(jnp.int32)
    residue = mode_index[:, None] * (2 * pix_index + 1)[None, :] % (2 * npix)
    phases = jnp.pi * residue.astype(jnp.float32) / npix.astype(jnp.float32)
    inside = pix_index[None, :] < npix
    weight = jnp.where(mode_index == 0, 1.0, 2.0).astype(jnp.float32)[:, None] / math.sqrt(2 * M)
    cos_part = jnp.where(inside, weight * jnp.cos(phases), 0.0)
    sin_part = jnp.where(inside, -weight * jnp.sin(phases), 0.0)
    return jnp.stack([cos_part, sin_part], axis=0).astype(jnp.bfloat16)

def reference(harmonics, mixing, beam_window, prior_inv, legendre, inv_noise, mode_index, cycle_pixels):
    degrees = jnp.arange(L).astype(jnp.int32)
    band_limit = L * cycle_pixels // PIX - 1
    filter_bank = jnp.where(degrees[None, :] <= band_limit[:, None], beam_window, 0.0)
    coeffs = harmonics.astype(jnp.float32)
    mixture = lax.optimization_barrier(jnp.sum(mixing[:, None, :, None, None] * coeffs[None], axis=2)) * filter_bank[:, None, None, :]
    channel_harmonic_coeffs = mixture.astype(jnp.bfloat16).transpose(2, 0, 1, 3).reshape(M, 2 * NCH, L)

    def forward_one(operands):
        rows_mode, table_mode = operands
        return jnp.dot(rows_mode, table_mode, preferred_element_type=jnp.float32)
    cycle_spectra = lax.map(forward_one, (channel_harmonic_coeffs, legendre)).astype(jnp.bfloat16)
    by_channel = cycle_spectra.reshape(M, NCH, 2, R).transpose(1, 3, 2, 0).reshape(NCH, R, 2 * M)

    def channel_sweep(operands):
        spectra, noise_rows, npix = operands
        table = dft_table(mode_index, npix).reshape(2 * M, PIX)
        sky_map = jnp.dot(spectra, table, preferred_element_type=jnp.float32)
        noisy_map = (noise_rows.astype(jnp.float32) * sky_map).astype(jnp.bfloat16)
        return jnp.dot(table, noisy_map.T, preferred_element_type=jnp.float32).astype(jnp.bfloat16)
    mode_spectra = lax.map(channel_sweep, (by_channel, inv_noise, cycle_pixels))
    mode_wise = mode_spectra.reshape(NCH, 2, M, R).transpose(2, 0, 1, 3).reshape(M, 2 * NCH, R)

    def backward_one(operands):
        rows_mode, table_mode = operands
        return jnp.dot(rows_mode, table_mode.T, preferred_element_type=jnp.float32)
    harmonic_back = lax.map(backward_one, (mode_wise, legendre)).reshape(M, NCH, 2, L)
    weighted = harmonic_back * filter_bank[None, :, None, :]
    transposed = jnp.einsum('ck,mcil->ikml', mixing, weighted, precision=lax.Precision.HIGHEST)
    return prior_inv[None, :, None, :] * coeffs + transposed
```

```python
import functools
import math

import jax
import jax.numpy as jnp
from jax import lax
from jax.experimental import pallas as pl
from jax.experimental.pallas import tpu as pltpu
from jax.sharding import PartitionSpec as P

MIB = 1 << 20
LANES = 128
ROWS = 8


def whole(space=pltpu.VMEM):
    return pl.BlockSpec(memory_space=space)


def filter_row(beam_ref, npix_ref, channel, degrees, total_deg, pixels):
    band_limit = total_deg * npix_ref[channel] // pixels - 1
    return jnp.where(degrees <= band_limit, beam_ref[pl.ds(channel, 1), :], 0.0)


def degrees_of(shape, chan_pos):
    return chan_pos * shape[-1] + lax.broadcasted_iota(jnp.int32, shape, len(shape) - 1)


def forward_body(chans, slots, pixels, npix_ref, mix_ref, harm_ref, beam_ref, leg_ref, *rest):
    outs, rows_ref = rest[:chans], rest[chans]
    step = pl.program_id(0)

    @pl.when(step == 0)
    def _():
        chan_pos = lax.axis_index("chan")
        local_deg = beam_ref.shape[1]
        degrees = degrees_of((1, local_deg), chan_pos)
        comps = [harm_ref[k].astype(jnp.float32) for k in range(harm_ref.shape[0])]
        for s in range(chans):
            group = (chan_pos + s) % chans
            for j in range(slots):
                c = group * slots + j
                mixture = sum(mix_ref[k, c] * comps[k] for k in range(len(comps)))
                filt = filter_row(beam_ref, npix_ref, c, degrees, local_deg * chans, pixels)
                rows_ref[pl.ds(s * ROWS + 2 * j, 2), :] = mixture * filt
            rest_rows = ROWS - 2 * slots
            rows_ref[pl.ds(s * ROWS + 2 * slots, rest_rows), :] = jnp.zeros(
                (rest_rows, local_deg), jnp.float32
            )

    rows = rows_ref[...].astype(jnp.bfloat16)
    partial = jnp.dot(rows, leg_ref[0], preferred_element_type=jnp.float32)
    for s in range(chans):
        outs[s][...] = partial[s * ROWS : (s + 1) * ROWS].astype(jnp.bfloat16)


def forward(npix, mixing_t, harm, beam, legendre, chans, slots, pixels, block):
    _, local_deg, cycles = legendre.shape
    return pl.pallas_call(
        functools.partial(forward_body, chans, slots, pixels),
        grid=(cycles // block,),
        in_specs=[
            whole(pltpu.SMEM),
            whole(pltpu.SMEM),
            whole(),
            whole(),
            pl.BlockSpec((1, local_deg, block), lambda r: (0, 0, r)),
        ],
        out_specs=[pl.BlockSpec((ROWS, block), lambda r: (0, r))] * chans,
        out_shape=[jax.ShapeDtypeStruct((ROWS, cycles), jnp.bfloat16)] * chans,
        scratch_shapes=[pltpu.VMEM((chans * ROWS, local_deg), jnp.float32)],
        compiler_params=pltpu.CompilerParams(vmem_limit_bytes=16 * MIB),
        cost_estimate=pl.CostEstimate(
            flops=2 * chans * ROWS * local_deg * cycles,
            bytes_accessed=2 * local_deg * cycles,
            transcendentals=0,
        ),
        name="forward",
    )(npix, mixing_t, harm, beam, legendre)


def gather_body(*refs):
    out_ref = refs[-1]
    total = refs[0][...].astype(jnp.float32)
    for ref in refs[1:-1]:
        total = total + ref[...].astype(jnp.float32)
    total = total.astype(jnp.bfloat16)
    for b in range(out_ref.shape[0]):
        out_ref[b] = total[:, b * LANES : (b + 1) * LANES]


def add_parts(parts):
    cycles = parts[0].shape[1]
    return pl.pallas_call(
        gather_body,
        in_specs=[whole()] * len(parts),
        out_specs=whole(),
        out_shape=jax.ShapeDtypeStruct((cycles // LANES, ROWS, LANES), jnp.bfloat16),
        compiler_params=pltpu.CompilerParams(vmem_limit_bytes=8 * MIB),
        name="add_parts",
    )(*parts)


def table_body(slots, npix_ref, mode_ref, out_ref):
    chan_pos = lax.axis_index("chan")
    modes = mode_ref[...]
    mode_count = modes.shape[0]
    pixels = out_ref.shape[2]
    coarse_count = pixels // LANES
    weight = jnp.where(modes == 0, 1.0, 2.0).astype(jnp.float32) / math.sqrt(2 * mode_count)
    lane = lax.broadcasted_iota(jnp.int32, (mode_count, LANES), 1)
    quarter = pixels // 4
    for j in range(slots):
        npix = npix_ref[chan_pos * slots + j]
        scale = jnp.float32(jnp.pi) / npix.astype(jnp.float32)
        fine_phase = ((modes * (2 * lane + 1)) & (2 * npix - 1)).astype(jnp.float32) * scale
        coarse_phase = ((modes * (2 * LANES * lane)) & (2 * npix - 1)).astype(jnp.float32) * scale
        fine_cos = jnp.cos(fine_phase) * weight
        fine_sin = jnp.sin(fine_phase) * weight
        coarse_cos = jnp.cos(coarse_phase)
        coarse_sin = jnp.sin(coarse_phase)
        for q in range(4):

            @pl.when(q * quarter < npix)
            def _():
                for a in range(q * coarse_count // 4, (q + 1) * coarse_count // 4):
                    cc = coarse_cos[:, a : a + 1]
                    cs = coarse_sin[:, a : a + 1]
                    cols = slice(a * LANES, (a + 1) * LANES)
                    cos_part = cc * fine_cos - cs * fine_sin
                    sin_part = -(cs * fine_cos + cc * fine_sin)
                    out_ref[j, :mode_count, cols] = cos_part.astype(jnp.bfloat16)
                    out_ref[j, mode_count:, cols] = sin_part.astype(jnp.bfloat16)


def make_tables(npix, modes, slots, pixels):
    mode_count = modes.shape[0]
    return pl.pallas_call(
        functools.partial(table_body, slots),
        in_specs=[whole(pltpu.SMEM), whole()],
        out_specs=whole(),
        out_shape=jax.ShapeDtypeStruct((slots, 2 * mode_count, pixels), jnp.bfloat16),
        compiler_params=pltpu.CompilerParams(vmem_limit_bytes=16 * MIB),
        cost_estimate=pl.CostEstimate(
            flops=10 * slots * mode_count * pixels,
            bytes_accessed=4 * slots * mode_count * pixels,
            transcendentals=4 * slots * mode_count * LANES,
        ),
        name="make_tables",
    )(npix, modes)


def middle_body(slots, block, npix_ref, spec_ref, table_ref, noise_ref, out_ref, full_ref, turned_ref, acc_ref):
    j = pl.program_id(0)
    p = pl.program_id(1)
    last = pl.num_programs(1) - 1
    mode_count = spec_ref.shape[0]
    flat = mode_count * ROWS

    @pl.when((j == 0) & (p == 0))
    def _():
        full_ref[...] = spec_ref[...].reshape(flat, LANES).astype(jnp.float32)
        for s in range(slots):
            halves = [full_ref[pl.ds(2 * s + i, mode_count, stride=ROWS), :] for i in range(2)]
            turned_ref[s] = jnp.concatenate(halves, axis=0).T.astype(jnp.bfloat16)
        full_ref[...] = jnp.zeros((flat, LANES), jnp.float32)

    @pl.when(p == 0)
    def _():
        acc_ref[...] = jnp.zeros(acc_ref.shape, jnp.float32)

    @pl.when(p * block < npix_ref[j])
    def _():
        table = table_ref[0]
        sky = jnp.dot(turned_ref[j], table, preferred_element_type=jnp.float32)
        noisy = (noise_ref[0].astype(jnp.float32) * sky).astype(jnp.bfloat16)
        acc_ref[...] += lax.dot_general(
            table, noisy, (((1,), (1,)), ((), ())), preferred_element_type=jnp.float32
        )

    @pl.when(p == last)
    def _():
        for i in range(2):
            full_ref[pl.ds(2 * j + i, mode_count, stride=ROWS), :] = acc_ref[
                i * mode_count : (i + 1) * mode_count
            ]

    @pl.when((p == last) & (j == slots - 1))
    def _():
        out_ref[...] = full_ref[...].reshape(mode_count, ROWS, LANES).astype(jnp.bfloat16)


def middle(npix_own, spectra, tables, inv_noise, block):
    slots, cycle_dev, pixels = inv_noise.shape
    mode_count = spectra.shape[0]

    def at(j, p, npix_ref):
        return (j, 0, jnp.minimum(p, npix_ref[j] // block - 1))

    return pl.pallas_call(
        functools.partial(middle_body, slots, block),
        grid_spec=pltpu.PrefetchScalarGridSpec(
            num_scalar_prefetch=1,
            grid=(slots, pixels // block),
            in_specs=[
                whole(),
                pl.BlockSpec((1, 2 * mode_count, block), at),
                pl.BlockSpec((1, cycle_dev, block), at),
            ],
            out_specs=whole(),
            scratch_shapes=[
                pltpu.VMEM((mode_count * ROWS, LANES), jnp.float32),
                pltpu.VMEM((slots, cycle_dev, 2 * mode_count), jnp.bfloat16),
                pltpu.VMEM((2 * mode_count, cycle_dev), jnp.float32),
            ],
        ),
        out_shape=jax.ShapeDtypeStruct(spectra.shape, jnp.bfloat16),
        compiler_params=pltpu.CompilerParams(vmem_limit_bytes=16 * MIB),
        name="middle",
    )(npix_own, spectra, tables, inv_noise)


def backward_body(chans, slots, pixels, npix_ref, mix_ref, harm_ref, beam_ref, prior_ref, leg_ref, *rest):
    parts, out_ref, acc_ref = rest[:chans], rest[chans], rest[chans + 1]
    step = pl.program_id(0)

    @pl.when(step == 0)
    def _():
        acc_ref[...] = jnp.zeros(acc_ref.shape, jnp.float32)

    rows = [
        jnp.concatenate([part[b] for b in range(part.shape[0])], axis=1) for part in parts
    ]
    rows = jnp.concatenate(rows, axis=0)
    acc_ref[...] += lax.dot_general(
        rows, leg_ref[0], (((1,), (1,)), ((), ())), preferred_element_type=jnp.float32
    )

    @pl.when(step == pl.num_programs(0) - 1)
    def _():
        chan_pos = lax.axis_index("chan")
        local_deg = beam_ref.shape[1]
        degrees = degrees_of((1, local_deg), chan_pos)
        comps = harm_ref.shape[0]
        totals = [prior_ref[k : k + 1, :] * harm_ref[k].astype(jnp.float32) for k in range(comps)]
        for s in range(chans):
            group = (chan_pos + chans - s) % chans
            for j in range(slots):
                c = group * slots + j
                filt = filter_row(beam_ref, npix_ref, c, degrees, local_deg * chans, pixels)
                weighted = acc_ref[pl.ds(s * ROWS + 2 * j, 2), :] * filt
                for k in range(comps):
                    totals[k] = totals[k] + mix_ref[k, c] * weighted
        for k in range(comps):
            for i in range(2):
                out_ref[i, k] = totals[k][i : i + 1]


def backward(npix, mixing_t, harm, beam, prior, legendre, parts, slots, pixels, block):
    chans = len(parts)
    _, local_deg, cycles = legendre.shape
    comps = harm.shape[0]
    return pl.pallas_call(
        functools.partial(backward_body, chans, slots, pixels),
        grid=(cycles // block,),
        in_specs=[
            whole(pltpu.SMEM),
            whole(pltpu.SMEM),
            whole(),
            whole(),
            whole(),
            pl.BlockSpec((1, local_deg, block), lambda r: (0, 0, r)),
        ]
        + [pl.BlockSpec((block // LANES, ROWS, LANES), lambda r: (r, 0, 0))] * chans,
        out_specs=whole(),
        out_shape=jax.ShapeDtypeStruct((2, comps, 1, local_deg), jnp.float32),
        scratch_shapes=[pltpu.VMEM((chans * ROWS, local_deg), jnp.float32)],
        compiler_params=pltpu.CompilerParams(vmem_limit_bytes=16 * MIB),
        name="backward",
    )(npix, mixing_t, harm, beam, prior, legendre, *parts)


def on_device(
    harmonics, mixing, beam_window, prior_inv, legendre, inv_noise, mode_index, cycle_pixels
):
    chans = lax.axis_size("chan")
    chan_pos = lax.axis_index("chan")
    slots, _, pixels = inv_noise.shape
    mixing_t = mixing.T
    harm = harmonics[:, :, 0, :].transpose(1, 0, 2)

    def shift(x, s):
        return lax.ppermute(x, "chan", [(d, (d + s) % chans) for d in range(chans)])

    parts = forward(cycle_pixels, mixing_t, harm, beam_window, legendre, chans, slots, pixels, 2048)
    parts = [parts[0]] + [shift(parts[s], s) for s in range(1, chans)]
    tables = make_tables(cycle_pixels, mode_index[:, None], slots, pixels)
    chunks = add_parts(parts)
    spectra = lax.all_to_all(chunks, ("mset", "blk"), split_axis=0, concat_axis=0, tiled=True)
    own_pixels = lax.dynamic_slice_in_dim(cycle_pixels, chan_pos * slots, slots)
    returned = middle(own_pixels, spectra, tables, inv_noise, 2048)
    own = lax.all_to_all(returned, ("mset", "blk"), split_axis=0, concat_axis=0, tiled=True)
    gathered = [own] + [shift(own, s) for s in range(1, chans)]
    return backward(
        cycle_pixels, mixing_t, harm, beam_window, prior_inv, legendre, gathered, slots, pixels, 2048
    )


def solution(mesh):
    placed = (
        P(None, None, ("mset", "blk"), "chan"),
        P(),
        P(None, "chan"),
        P(None, "chan"),
        P(("mset", "blk"), "chan", None),
        P("chan", ("mset", "blk"), None),
        P(),
        P(),
    )
    return jax.shard_map(
        on_device,
        mesh=mesh,
        in_specs=placed,
        out_specs=P(None, None, ("mset", "blk"), "chan"),
        check_vma=False,
    )
```

```python
import functools
import math

import jax
import jax.numpy as jnp
from jax import lax
from jax.experimental import pallas as pl
from jax.experimental.pallas import tpu as pltpu
from jax.sharding import PartitionSpec as P

MIB = 1 << 20
LANES = 128
ROWS = 8


def whole(space=pltpu.VMEM):
    return pl.BlockSpec(memory_space=space)


def in_hbm(*arrays):
    return [pltpu.with_memory_space_constraint(x, pltpu.HBM) for x in arrays]


def filter_row(beam_ref, npix_ref, channel, degrees, total_deg, pixels):
    band_limit = total_deg * npix_ref[channel] // pixels - 1
    return jnp.where(degrees <= band_limit, beam_ref[pl.ds(channel, 1), :], 0.0)


def degrees_of(shape, chan_pos):
    return chan_pos * shape[-1] + lax.broadcasted_iota(jnp.int32, shape, len(shape) - 1)


def forward_body(chans, slots, pixels, npix_ref, mix_ref, harm_ref, beam_ref, leg_ref, *rest):
    outs, rows_ref = rest[:chans], rest[chans]
    step = pl.program_id(0)

    @pl.when(step == 0)
    def _():
        chan_pos = lax.axis_index("chan")
        local_deg = beam_ref.shape[1]
        degrees = degrees_of((1, local_deg), chan_pos)
        comps = [harm_ref[k].astype(jnp.float32) for k in range(harm_ref.shape[0])]
        for s in range(chans):
            group = (chan_pos + s) % chans
            for j in range(slots):
                c = group * slots + j
                mixture = sum(mix_ref[k, c] * comps[k] for k in range(len(comps)))
                filt = filter_row(beam_ref, npix_ref, c, degrees, local_deg * chans, pixels)
                rows_ref[pl.ds(s * ROWS + 2 * j, 2), :] = mixture * filt
            rest_rows = ROWS - 2 * slots
            rows_ref[pl.ds(s * ROWS + 2 * slots, rest_rows), :] = jnp.zeros(
                (rest_rows, local_deg), jnp.float32
            )

    rows = rows_ref[...].astype(jnp.bfloat16)
    partial = jnp.dot(rows, leg_ref[0], preferred_element_type=jnp.float32)
    for s in range(chans):
        outs[s][...] = partial[s * ROWS : (s + 1) * ROWS].astype(jnp.bfloat16)


def forward(npix, mixing_t, harm, beam, legendre, chans, slots, pixels, block):
    _, local_deg, cycles = legendre.shape
    return pl.pallas_call(
        functools.partial(forward_body, chans, slots, pixels),
        grid=(cycles // block,),
        in_specs=[
            whole(pltpu.SMEM),
            whole(pltpu.SMEM),
            whole(),
            whole(),
            pl.BlockSpec((1, local_deg, block), lambda r: (0, 0, r)),
        ],
        out_specs=[pl.BlockSpec((ROWS, block), lambda r: (0, r))] * chans,
        out_shape=[jax.ShapeDtypeStruct((ROWS, cycles), jnp.bfloat16)] * chans,
        scratch_shapes=[pltpu.VMEM((chans * ROWS, local_deg), jnp.float32)],
        compiler_params=pltpu.CompilerParams(vmem_limit_bytes=16 * MIB),
        cost_estimate=pl.CostEstimate(
            flops=2 * chans * ROWS * local_deg * cycles,
            bytes_accessed=2 * local_deg * cycles,
            transcendentals=0,
        ),
        name="forward",
    )(*in_hbm(npix, mixing_t, harm, beam, legendre))


def gather_body(*refs):
    out_ref = refs[-1]
    total = refs[0][...].astype(jnp.float32)
    for ref in refs[1:-1]:
        total = total + ref[...].astype(jnp.float32)
    total = total.astype(jnp.bfloat16)
    for b in range(out_ref.shape[0]):
        out_ref[b] = total[:, b * LANES : (b + 1) * LANES]


def add_parts(parts):
    cycles = parts[0].shape[1]
    return pl.pallas_call(
        gather_body,
        in_specs=[whole()] * len(parts),
        out_specs=whole(),
        out_shape=jax.ShapeDtypeStruct((cycles // LANES, ROWS, LANES), jnp.bfloat16),
        compiler_params=pltpu.CompilerParams(vmem_limit_bytes=8 * MIB),
        name="add_parts",
    )(*parts)


def table_body(slots, npix_ref, mode_ref, out_ref):
    chan_pos = lax.axis_index("chan")
    modes = mode_ref[...]
    mode_count = modes.shape[0]
    pixels = out_ref.shape[2]
    coarse_count = pixels // LANES
    weight = jnp.where(modes == 0, 1.0, 2.0).astype(jnp.float32) / math.sqrt(2 * mode_count)
    lane = lax.broadcasted_iota(jnp.int32, (mode_count, LANES), 1)
    quarter = pixels // 4
    for j in range(slots):
        npix = npix_ref[chan_pos * slots + j]
        scale = jnp.float32(jnp.pi) / npix.astype(jnp.float32)
        fine_phase = ((modes * (2 * lane + 1)) & (2 * npix - 1)).astype(jnp.float32) * scale
        coarse_phase = ((modes * (2 * LANES * lane)) & (2 * npix - 1)).astype(jnp.float32) * scale
        fine_cos = jnp.cos(fine_phase) * weight
        fine_sin = jnp.sin(fine_phase) * weight
        coarse_cos = jnp.cos(coarse_phase)
        coarse_sin = jnp.sin(coarse_phase)
        for q in range(4):

            @pl.when(q * quarter < npix)
            def _():
                for a in range(q * coarse_count // 4, (q + 1) * coarse_count // 4):
                    cc = coarse_cos[:, a : a + 1]
                    cs = coarse_sin[:, a : a + 1]
                    cols = slice(a * LANES, (a + 1) * LANES)
                    cos_part = cc * fine_cos - cs * fine_sin
                    sin_part = -(cs * fine_cos + cc * fine_sin)
                    out_ref[j, :mode_count, cols] = cos_part.astype(jnp.bfloat16)
                    out_ref[j, mode_count:, cols] = sin_part.astype(jnp.bfloat16)


def make_tables(npix, modes, slots, pixels):
    mode_count = modes.shape[0]
    return pl.pallas_call(
        functools.partial(table_body, slots),
        in_specs=[whole(pltpu.SMEM), whole()],
        out_specs=whole(),
        out_shape=pltpu.VMEM((slots, 2 * mode_count, pixels), jnp.bfloat16),
        compiler_params=pltpu.CompilerParams(vmem_limit_bytes=16 * MIB),
        cost_estimate=pl.CostEstimate(
            flops=10 * slots * mode_count * pixels,
            bytes_accessed=4 * slots * mode_count * pixels,
            transcendentals=4 * slots * mode_count * LANES,
        ),
        name="make_tables",
    )(npix, modes)


def middle_body(slots, block, npix_ref, spec_ref, table_ref, noise_ref, out_ref, full_ref, turned_ref, acc_ref):
    j = pl.program_id(0)
    p = pl.program_id(1)
    last = pl.num_programs(1) - 1
    mode_count = spec_ref.shape[0]
    flat = mode_count * ROWS

    @pl.when((j == 0) & (p == 0))
    def _():
        full_ref[...] = spec_ref[...].reshape(flat, LANES).astype(jnp.float32)
        for s in range(slots):
            halves = [full_ref[pl.ds(2 * s + i, mode_count, stride=ROWS), :] for i in range(2)]
            turned_ref[s] = jnp.concatenate(halves, axis=0).T.astype(jnp.bfloat16)
        full_ref[...] = jnp.zeros((flat, LANES), jnp.float32)

    @pl.when(p == 0)
    def _():
        acc_ref[...] = jnp.zeros(acc_ref.shape, jnp.float32)

    @pl.when(p * block < npix_ref[j])
    def _():
        table = table_ref[j, :, pl.ds(pl.multiple_of(p * block, block), block)]
        sky = jnp.dot(turned_ref[j], table, preferred_element_type=jnp.float32)
        noisy = (noise_ref[0].astype(jnp.float32) * sky).astype(jnp.bfloat16)
        acc_ref[...] += lax.dot_general(
            table, noisy, (((1,), (1,)), ((), ())), preferred_element_type=jnp.float32
        )

    @pl.when(p == last)
    def _():
        for i in range(2):
            full_ref[pl.ds(2 * j + i, mode_count, stride=ROWS), :] = acc_ref[
                i * mode_count : (i + 1) * mode_count
            ]

    @pl.when((p == last) & (j == slots - 1))
    def _():
        out_ref[...] = full_ref[...].reshape(mode_count, ROWS, LANES).astype(jnp.bfloat16)


def middle(npix_own, spectra, tables, inv_noise, block):
    slots, cycle_dev, pixels = inv_noise.shape
    mode_count = spectra.shape[0]

    def at(j, p, npix_ref):
        return (j, 0, jnp.minimum(p, npix_ref[j] // block - 1))

    return pl.pallas_call(
        functools.partial(middle_body, slots, block),
        grid_spec=pltpu.PrefetchScalarGridSpec(
            num_scalar_prefetch=1,
            grid=(slots, pixels // block),
            in_specs=[
                whole(),
                whole(),
                pl.BlockSpec((1, cycle_dev, block), at),
            ],
            out_specs=whole(),
            scratch_shapes=[
                pltpu.VMEM((mode_count * ROWS, LANES), jnp.float32),
                pltpu.VMEM((slots, cycle_dev, 2 * mode_count), jnp.bfloat16),
                pltpu.VMEM((2 * mode_count, cycle_dev), jnp.float32),
            ],
        ),
        out_shape=jax.ShapeDtypeStruct(spectra.shape, jnp.bfloat16),
        compiler_params=pltpu.CompilerParams(vmem_limit_bytes=16 * MIB),
        name="middle",
    )(npix_own, spectra, pltpu.with_memory_space_constraint(tables, pltpu.VMEM), *in_hbm(inv_noise))


def backward_body(chans, slots, pixels, npix_ref, mix_ref, harm_ref, beam_ref, prior_ref, leg_ref, *rest):
    parts, out_ref, acc_ref = rest[:chans], rest[chans], rest[chans + 1]
    step = pl.program_id(0)

    @pl.when(step == 0)
    def _():
        acc_ref[...] = jnp.zeros(acc_ref.shape, jnp.float32)

    rows = [
        jnp.concatenate([part[b] for b in range(part.shape[0])], axis=1) for part in parts
    ]
    rows = jnp.concatenate(rows, axis=0)
    acc_ref[...] += lax.dot_general(
        rows, leg_ref[0], (((1,), (1,)), ((), ())), preferred_element_type=jnp.float32
    )

    @pl.when(step == pl.num_programs(0) - 1)
    def _():
        chan_pos = lax.axis_index("chan")
        local_deg = beam_ref.shape[1]
        degrees = degrees_of((1, local_deg), chan_pos)
        comps = harm_ref.shape[0]
        totals = [prior_ref[k : k + 1, :] * harm_ref[k].astype(jnp.float32) for k in range(comps)]
        for s in range(chans):
            group = (chan_pos + chans - s) % chans
            for j in range(slots):
                c = group * slots + j
                filt = filter_row(beam_ref, npix_ref, c, degrees, local_deg * chans, pixels)
                weighted = acc_ref[pl.ds(s * ROWS + 2 * j, 2), :] * filt
                for k in range(comps):
                    totals[k] = totals[k] + mix_ref[k, c] * weighted
        for k in range(comps):
            for i in range(2):
                out_ref[i, k] = totals[k][i : i + 1]


def backward(npix, mixing_t, harm, beam, prior, legendre, parts, slots, pixels, block):
    chans = len(parts)
    _, local_deg, cycles = legendre.shape
    comps = harm.shape[0]
    return pl.pallas_call(
        functools.partial(backward_body, chans, slots, pixels),
        grid=(cycles // block,),
        in_specs=[
            whole(pltpu.SMEM),
            whole(pltpu.SMEM),
            whole(),
            whole(),
            whole(),
            pl.BlockSpec((1, local_deg, block), lambda r: (0, 0, r)),
        ]
        + [pl.BlockSpec((block // LANES, ROWS, LANES), lambda r: (r, 0, 0))] * chans,
        out_specs=whole(),
        out_shape=jax.ShapeDtypeStruct((2, comps, 1, local_deg), jnp.float32),
        scratch_shapes=[pltpu.VMEM((chans * ROWS, local_deg), jnp.float32)],
        compiler_params=pltpu.CompilerParams(vmem_limit_bytes=16 * MIB),
        name="backward",
    )(npix, mixing_t, harm, beam, prior, legendre, *parts)


def on_device(
    harmonics, mixing, beam_window, prior_inv, legendre, inv_noise, mode_index, cycle_pixels
):
    chans = lax.axis_size("chan")
    chan_pos = lax.axis_index("chan")
    slots, _, pixels = inv_noise.shape
    mixing_t = mixing.T
    harm = harmonics[:, :, 0, :].transpose(1, 0, 2)

    def shift(x, s):
        return lax.ppermute(x, "chan", [(d, (d + s) % chans) for d in range(chans)])

    parts = forward(cycle_pixels, mixing_t, harm, beam_window, legendre, chans, slots, pixels, 2048)
    parts = [parts[0]] + [shift(parts[s], s) for s in range(1, chans)]
    tables = make_tables(cycle_pixels, mode_index[:, None], slots, pixels)
    own_pixels = lax.dynamic_slice_in_dim(cycle_pixels, chan_pos * slots, slots)
    tables, own_pixels, parts = lax.optimization_barrier((tables, own_pixels, parts))
    chunks = add_parts(parts)
    spectra = lax.all_to_all(chunks, ("mset", "blk"), split_axis=0, concat_axis=0, tiled=True)
    returned = middle(own_pixels, spectra, tables, inv_noise, 2048)
    own = lax.all_to_all(returned, ("mset", "blk"), split_axis=0, concat_axis=0, tiled=True)
    gathered = [own] + [shift(own, s) for s in range(1, chans)]
    return backward(
        cycle_pixels, mixing_t, harm, beam_window, prior_inv, legendre, gathered, slots, pixels, 2048
    )


def solution(mesh):
    placed = (
        P(None, None, ("mset", "blk"), "chan"),
        P(),
        P(None, "chan"),
        P(None, "chan"),
        P(("mset", "blk"), "chan", None),
        P("chan", ("mset", "blk"), None),
        P(),
        P(),
    )
    return jax.shard_map(
        on_device,
        mesh=mesh,
        in_specs=placed,
        out_specs=P(None, None, ("mset", "blk"), "chan"),
        check_vma=False,
    )
```

```python
import functools
import math

import jax
import jax.numpy as jnp
from jax import lax
from jax.experimental import pallas as pl
from jax.experimental.pallas import tpu as pltpu
from jax.sharding import PartitionSpec as P

MIB = 1 << 20
LANES = 128
ROWS = 8
QUARTERS = 4


def whole(space=pltpu.VMEM):
    return pl.BlockSpec(memory_space=space)


def in_hbm(*arrays):
    return [pltpu.with_memory_space_constraint(x, pltpu.HBM) for x in arrays]


def in_vmem(*arrays):
    return [pltpu.with_memory_space_constraint(x, pltpu.VMEM) for x in arrays]


def filter_row(beam_ref, npix_ref, channel, degrees, total_deg, pixels):
    band_limit = total_deg * npix_ref[channel] // pixels - 1
    return jnp.where(degrees <= band_limit, beam_ref[pl.ds(channel, 1), :], 0.0)


def degrees_of(shape, chan_pos):
    return chan_pos * shape[-1] + lax.broadcasted_iota(jnp.int32, shape, len(shape) - 1)


def forward_body(chans, slots, pixels, steps, npix_any, mix_any, harm_any, beam_any, leg_any, *rest):
    outs = rest[:chans]
    npix_ref, mix_ref, harm_ref, beam_ref, rows_ref, leg_ref, sems, small = rest[chans:]
    small_copies = [
        pltpu.make_async_copy(src, dst, small.at[n])
        for n, (src, dst) in enumerate(
            [
                (npix_any, npix_ref),
                (mix_any, mix_ref),
                (harm_any, harm_ref),
                (beam_any, beam_ref),
            ]
        )
    ]
    local_deg, cycles = leg_ref.shape
    block = cycles // steps
    copies = [
        pltpu.make_async_copy(
            leg_any.at[0, :, pl.ds(q * block, block)],
            leg_ref.at[:, pl.ds(q * block, block)],
            sems.at[q],
        )
        for q in range(steps)
    ]
    for copy in small_copies + copies:
        copy.start()
    for copy in small_copies:
        copy.wait()
    chan_pos = lax.axis_index("chan")
    degrees = degrees_of((1, local_deg), chan_pos)
    comps = [harm_ref[k].astype(jnp.float32) for k in range(harm_ref.shape[0])]
    for s in range(chans):
        group = (chan_pos + s) % chans
        for j in range(slots):
            c = group * slots + j
            mixture = sum(mix_ref[k, c] * comps[k] for k in range(len(comps)))
            filt = filter_row(beam_ref, npix_ref, c, degrees, local_deg * chans, pixels)
            rows_ref[pl.ds(s * ROWS + 2 * j, 2), :] = mixture * filt
        rest_rows = ROWS - 2 * slots
        rows_ref[pl.ds(s * ROWS + 2 * slots, rest_rows), :] = jnp.zeros(
            (rest_rows, local_deg), jnp.float32
        )
    rows = rows_ref[...].astype(jnp.bfloat16)
    used = 2 * slots
    for q in range(steps):
        copies[q].wait()
        partial = jnp.dot(
            rows, leg_ref[:, q * block : (q + 1) * block], preferred_element_type=jnp.float32
        )
        for s in range(chans):
            outs[s][q * used : (q + 1) * used, :] = partial[s * ROWS : s * ROWS + used].astype(
                jnp.bfloat16
            )


def forward(npix, mixing_t, harm, beam, legendre, chans, slots, pixels):
    _, local_deg, cycles = legendre.shape
    used = 2 * slots
    return pl.pallas_call(
        functools.partial(forward_body, chans, slots, pixels, QUARTERS),
        in_specs=[whole(pl.ANY)] * 5,
        out_specs=[whole()] * chans,
        out_shape=[jax.ShapeDtypeStruct((QUARTERS * used, cycles // QUARTERS), jnp.bfloat16)] * chans,
        scratch_shapes=[
            pltpu.SMEM(npix.shape, npix.dtype),
            pltpu.SMEM(mixing_t.shape, mixing_t.dtype),
            pltpu.VMEM(harm.shape, harm.dtype),
            pltpu.VMEM(beam.shape, beam.dtype),
            pltpu.VMEM((chans * ROWS, local_deg), jnp.float32),
            pltpu.VMEM((local_deg, cycles), jnp.bfloat16),
            pltpu.SemaphoreType.DMA((QUARTERS,)),
            pltpu.SemaphoreType.DMA((4,)),
        ],
        compiler_params=pltpu.CompilerParams(vmem_limit_bytes=16 * MIB),
        cost_estimate=pl.CostEstimate(
            flops=2 * chans * ROWS * local_deg * cycles,
            bytes_accessed=2 * local_deg * cycles,
            transcendentals=0,
        ),
        name="forward",
    )(*in_hbm(npix, mixing_t, harm, beam, legendre))


def gather_body(used, *refs):
    out_ref = refs[-1]
    total = refs[0][...].astype(jnp.float32)
    for ref in refs[1:-1]:
        total = total + ref[...].astype(jnp.float32)
    width = total.shape[1]
    per = width // LANES
    pad = jnp.zeros((ROWS - used, width), jnp.float32)
    for q in range(total.shape[0] // used):
        part = jnp.concatenate([total[q * used : (q + 1) * used], pad], axis=0).astype(jnp.bfloat16)
        for b in range(per):
            out_ref[q * per + b] = part[:, b * LANES : (b + 1) * LANES]


def add_parts(parts):
    height, width = parts[0].shape
    used = height // QUARTERS
    return pl.pallas_call(
        functools.partial(gather_body, used),
        in_specs=[whole()] * len(parts),
        out_specs=whole(),
        out_shape=jax.ShapeDtypeStruct((QUARTERS * width // LANES, ROWS, LANES), jnp.bfloat16),
        compiler_params=pltpu.CompilerParams(vmem_limit_bytes=8 * MIB),
        name="add_parts",
    )(*parts)


def table_body(slots, npix_ref, mode_ref, noise_any, out_ref, noise_ref, sems):
    chan_pos = lax.axis_index("chan")
    modes = mode_ref[...]
    mode_count = modes.shape[0]
    pixels = out_ref.shape[2]
    coarse_count = pixels // LANES
    quarter = pixels // 4

    def noise_copy(j, q):
        cols = pl.ds(q * quarter, quarter)
        return pltpu.make_async_copy(noise_any.at[j, :, cols], noise_ref.at[j, :, cols], sems.at[j, q])

    for j in range(slots):
        for q in range(4):

            @pl.when(q * quarter < npix_ref[chan_pos * slots + j])
            def _():
                noise_copy(j, q).start()

    weight = jnp.where(modes == 0, 1.0, 2.0).astype(jnp.float32) / math.sqrt(2 * mode_count)
    lane = lax.broadcasted_iota(jnp.int32, (mode_count, LANES), 1)
    for j in range(slots):
        npix = npix_ref[chan_pos * slots + j]
        scale = jnp.float32(jnp.pi) / npix.astype(jnp.float32)
        fine_phase = ((modes * (2 * lane + 1)) & (2 * npix - 1)).astype(jnp.float32) * scale
        coarse_phase = ((modes * (2 * LANES * lane)) & (2 * npix - 1)).astype(jnp.float32) * scale
        fine_cos = jnp.cos(fine_phase) * weight
        fine_sin = jnp.sin(fine_phase) * weight
        coarse_cos = jnp.cos(coarse_phase)
        coarse_sin = jnp.sin(coarse_phase)
        for q in range(4):

            @pl.when(q * quarter < npix)
            def _():
                for a in range(q * coarse_count // 4, (q + 1) * coarse_count // 4):
                    cc = coarse_cos[:, a : a + 1]
                    cs = coarse_sin[:, a : a + 1]
                    cols = slice(a * LANES, (a + 1) * LANES)
                    cos_part = cc * fine_cos - cs * fine_sin
                    sin_part = -(cs * fine_cos + cc * fine_sin)
                    out_ref[j, :mode_count, cols] = cos_part.astype(jnp.bfloat16)
                    out_ref[j, mode_count:, cols] = sin_part.astype(jnp.bfloat16)

    for j in range(slots):
        for q in range(4):

            @pl.when(q * quarter < npix_ref[chan_pos * slots + j])
            def _():
                noise_copy(j, q).wait()


def make_tables(npix, modes, inv_noise):
    slots, _, pixels = inv_noise.shape
    mode_count = modes.shape[0]
    return pl.pallas_call(
        functools.partial(table_body, slots),
        in_specs=[whole(pltpu.SMEM), whole(), whole(pl.ANY)],
        out_specs=[whole(), whole()],
        out_shape=[
            pltpu.VMEM((slots, 2 * mode_count, pixels), jnp.bfloat16),
            pltpu.VMEM(inv_noise.shape, jnp.bfloat16),
        ],
        scratch_shapes=[pltpu.SemaphoreType.DMA((slots, 4))],
        compiler_params=pltpu.CompilerParams(vmem_limit_bytes=16 * MIB),
        cost_estimate=pl.CostEstimate(
            flops=10 * slots * mode_count * pixels,
            bytes_accessed=4 * slots * mode_count * pixels,
            transcendentals=4 * slots * mode_count * LANES,
        ),
        name="make_tables",
    )(npix, modes, *in_hbm(inv_noise))


def middle_body(npix_ref, spec_ref, table_ref, noise_ref, out_ref, full_ref, turned_ref):
    mode_count = spec_ref.shape[0]
    slots, _, pixels = noise_ref.shape
    flat = mode_count * ROWS
    chan_pos = lax.axis_index("chan")
    full_ref[...] = spec_ref[...].reshape(flat, LANES).astype(jnp.float32)
    for s in range(slots):
        halves = [full_ref[pl.ds(2 * s + i, mode_count, stride=ROWS), :] for i in range(2)]
        turned_ref[s] = jnp.concatenate(halves, axis=0).T.astype(jnp.bfloat16)
    full_ref[...] = jnp.zeros((flat, LANES), jnp.float32)

    def one_channel(j, carry):
        spectra = turned_ref[j]
        npix = npix_ref[chan_pos * slots + j]
        for width in (pixels // 4, pixels // 2, pixels):

            @pl.when(npix == width)
            def _():
                table = table_ref[j, :, :width]
                sky = jnp.dot(spectra, table, preferred_element_type=jnp.float32)
                noisy = (noise_ref[j, :, :width].astype(jnp.float32) * sky).astype(jnp.bfloat16)
                back = lax.dot_general(
                    table, noisy, (((1,), (1,)), ((), ())), preferred_element_type=jnp.float32
                )
                for i in range(2):
                    full_ref[pl.ds(2 * j + i, mode_count, stride=ROWS), :] = back[
                        i * mode_count : (i + 1) * mode_count
                    ]

        return carry

    lax.fori_loop(0, slots, one_channel, 0)
    out_ref[...] = full_ref[...].reshape(mode_count, ROWS, LANES).astype(jnp.bfloat16)


def middle(npix, spectra, tables, noise):
    slots, cycle_dev, _ = noise.shape
    mode_count = spectra.shape[0]
    return pl.pallas_call(
        middle_body,
        in_specs=[whole(pltpu.SMEM), whole(), whole(), whole()],
        out_specs=whole(),
        out_shape=jax.ShapeDtypeStruct(spectra.shape, jnp.bfloat16),
        scratch_shapes=[
            pltpu.VMEM((mode_count * ROWS, LANES), jnp.float32),
            pltpu.VMEM((slots, cycle_dev, 2 * mode_count), jnp.bfloat16),
        ],
        compiler_params=pltpu.CompilerParams(vmem_limit_bytes=20 * MIB),
        name="middle",
    )(npix, spectra, *in_vmem(tables, noise))


def backward_body(chans, slots, pixels, npix_ref, mix_ref, harm_ref, beam_ref, prior_ref, leg_ref, *rest):
    parts, out_ref, acc_ref = rest[:chans], rest[chans], rest[chans + 1]
    rows = [
        jnp.concatenate([part[b] for b in range(part.shape[0])], axis=1) for part in parts
    ]
    rows = jnp.concatenate(rows, axis=0)
    acc_ref[...] = lax.dot_general(
        leg_ref[0], rows, (((1,), (1,)), ((), ())), preferred_element_type=jnp.float32
    ).T
    chan_pos = lax.axis_index("chan")
    local_deg = beam_ref.shape[1]
    degrees = degrees_of((1, local_deg), chan_pos)
    comps = harm_ref.shape[0]
    totals = [prior_ref[k : k + 1, :] * harm_ref[k].astype(jnp.float32) for k in range(comps)]
    for s in range(chans):
        group = (chan_pos + chans - s) % chans
        for j in range(slots):
            c = group * slots + j
            filt = filter_row(beam_ref, npix_ref, c, degrees, local_deg * chans, pixels)
            weighted = acc_ref[pl.ds(s * ROWS + 2 * j, 2), :] * filt
            for k in range(comps):
                totals[k] = totals[k] + mix_ref[k, c] * weighted
    for k in range(comps):
        for i in range(2):
            out_ref[i, k] = totals[k][i : i + 1]


def backward(npix, mixing_t, harm, beam, prior, legendre, parts, slots, pixels):
    chans = len(parts)
    local_deg = legendre.shape[1]
    comps = harm.shape[0]
    return pl.pallas_call(
        functools.partial(backward_body, chans, slots, pixels),
        in_specs=[whole(pltpu.SMEM), whole(pltpu.SMEM)] + [whole()] * (4 + chans),
        out_specs=whole(),
        out_shape=jax.ShapeDtypeStruct((2, comps, 1, local_deg), jnp.float32),
        scratch_shapes=[pltpu.VMEM((chans * ROWS, local_deg), jnp.float32)],
        compiler_params=pltpu.CompilerParams(vmem_limit_bytes=16 * MIB),
        name="backward",
    )(npix, mixing_t, harm, beam, prior, legendre, *parts)


def on_device(
    harmonics, mixing, beam_window, prior_inv, legendre, inv_noise, mode_index, cycle_pixels
):
    chans = lax.axis_size("chan")
    slots, _, pixels = inv_noise.shape
    mixing_t = mixing.T
    harm = harmonics[:, :, 0, :].transpose(1, 0, 2)

    def shift(x, s):
        return lax.ppermute(x, "chan", [(d, (d + s) % chans) for d in range(chans)])

    parts = forward(
        cycle_pixels, mixing_t, harm, beam_window, legendre, chans, slots, pixels
    )
    parts = [parts[0]] + [shift(parts[s], s) for s in range(1, chans)]
    tables, noise = make_tables(cycle_pixels, mode_index[:, None], inv_noise)
    tables, noise, parts = lax.optimization_barrier((tables, noise, parts))
    chunks = add_parts(parts)
    spectra = lax.all_to_all(chunks, ("mset", "blk"), split_axis=0, concat_axis=0, tiled=True)
    returned = middle(cycle_pixels, spectra, tables, noise)
    own = lax.all_to_all(returned, ("mset", "blk"), split_axis=0, concat_axis=0, tiled=True)
    gathered = [own] + [shift(own, s) for s in range(1, chans)]
    return backward(
        cycle_pixels, mixing_t, harm, beam_window, prior_inv, legendre, gathered, slots, pixels
    )


def solution(mesh):
    placed = (
        P(None, None, ("mset", "blk"), "chan"),
        P(),
        P(None, "chan"),
        P(None, "chan"),
        P(("mset", "blk"), "chan", None),
        P("chan", ("mset", "blk"), None),
        P(),
        P(),
    )
    return jax.shard_map(
        on_device,
        mesh=mesh,
        in_specs=placed,
        out_specs=P(None, None, ("mset", "blk"), "chan"),
        check_vma=False,
    )
```

```python
import functools
import math

import jax
import jax.numpy as jnp
from jax import lax
from jax.experimental import pallas as pl
from jax.experimental.pallas import tpu as pltpu
from jax.sharding import PartitionSpec as P

MIB = 1 << 20
LANES = 128
ROWS = 8
QUARTERS = 4
FINE = 64
SINE = [(-1) ** n / math.factorial(2 * n + 1) for n in range(6)]


def whole(space=pltpu.VMEM):
    return pl.BlockSpec(memory_space=space)


def in_hbm(*arrays):
    return [pltpu.with_memory_space_constraint(x, pltpu.HBM) for x in arrays]


def in_vmem(*arrays):
    return [pltpu.with_memory_space_constraint(x, pltpu.VMEM) for x in arrays]


def filter_row(beam_ref, npix_ref, channel, degrees, total_deg, pixels):
    band_limit = total_deg * npix_ref[channel] // pixels - 1
    return jnp.where(degrees <= band_limit, beam_ref[pl.ds(channel, 1), :], 0.0)


def degrees_of(shape, chan_pos):
    return chan_pos * shape[-1] + lax.broadcasted_iota(jnp.int32, shape, len(shape) - 1)


def forward_body(chans, slots, pixels, steps, npix_any, mix_any, harm_any, beam_any, leg_any, *rest):
    outs = rest[:chans]
    npix_ref, mix_ref, harm_ref, beam_ref, rows_ref, leg_ref, sems, small = rest[chans:]
    small_copies = [
        pltpu.make_async_copy(src, dst, small.at[n])
        for n, (src, dst) in enumerate(
            [
                (npix_any, npix_ref),
                (mix_any, mix_ref),
                (harm_any, harm_ref),
                (beam_any, beam_ref),
            ]
        )
    ]
    local_deg, cycles = leg_ref.shape
    block = cycles // steps
    copies = [
        pltpu.make_async_copy(
            leg_any.at[0, :, pl.ds(q * block, block)],
            leg_ref.at[:, pl.ds(q * block, block)],
            sems.at[q],
        )
        for q in range(steps)
    ]
    for copy in small_copies + copies:
        copy.start()
    for copy in small_copies:
        copy.wait()
    chan_pos = lax.axis_index("chan")
    degrees = degrees_of((1, local_deg), chan_pos)
    comps = [harm_ref[k].astype(jnp.float32) for k in range(harm_ref.shape[0])]
    for s in range(chans):
        group = (chan_pos + s) % chans
        for j in range(slots):
            c = group * slots + j
            mixture = sum(mix_ref[k, c] * comps[k] for k in range(len(comps)))
            filt = filter_row(beam_ref, npix_ref, c, degrees, local_deg * chans, pixels)
            rows_ref[pl.ds(s * ROWS + 2 * j, 2), :] = mixture * filt
        rest_rows = ROWS - 2 * slots
        rows_ref[pl.ds(s * ROWS + 2 * slots, rest_rows), :] = jnp.zeros(
            (rest_rows, local_deg), jnp.float32
        )
    rows = rows_ref[...].astype(jnp.bfloat16)
    used = 2 * slots
    for q in range(steps):
        copies[q].wait()
        partial = jnp.dot(
            rows, leg_ref[:, q * block : (q + 1) * block], preferred_element_type=jnp.float32
        )
        for s in range(chans):
            outs[s][q * used : (q + 1) * used, :] = partial[s * ROWS : s * ROWS + used].astype(
                jnp.bfloat16
            )


def forward(npix, mixing_t, harm, beam, legendre, chans, slots, pixels):
    _, local_deg, cycles = legendre.shape
    used = 2 * slots
    return pl.pallas_call(
        functools.partial(forward_body, chans, slots, pixels, QUARTERS),
        in_specs=[whole(pl.ANY)] * 5,
        out_specs=[whole()] * chans,
        out_shape=[jax.ShapeDtypeStruct((QUARTERS * used, cycles // QUARTERS), jnp.bfloat16)] * chans,
        scratch_shapes=[
            pltpu.SMEM(npix.shape, npix.dtype),
            pltpu.SMEM(mixing_t.shape, mixing_t.dtype),
            pltpu.VMEM(harm.shape, harm.dtype),
            pltpu.VMEM(beam.shape, beam.dtype),
            pltpu.VMEM((chans * ROWS, local_deg), jnp.float32),
            pltpu.VMEM((local_deg, cycles), jnp.bfloat16),
            pltpu.SemaphoreType.DMA((QUARTERS,)),
            pltpu.SemaphoreType.DMA((4,)),
        ],
        compiler_params=pltpu.CompilerParams(vmem_limit_bytes=16 * MIB),
        cost_estimate=pl.CostEstimate(
            flops=2 * chans * ROWS * local_deg * cycles,
            bytes_accessed=2 * local_deg * cycles,
            transcendentals=0,
        ),
        name="forward",
    )(*in_hbm(npix, mixing_t, harm, beam, legendre))


def gather_body(used, *refs):
    out_ref = refs[-1]
    total = refs[0][...].astype(jnp.float32)
    for ref in refs[1:-1]:
        total = total + ref[...].astype(jnp.float32)
    width = total.shape[1]
    per = width // LANES
    pad = jnp.zeros((ROWS - used, width), jnp.float32)
    for q in range(total.shape[0] // used):
        part = jnp.concatenate([total[q * used : (q + 1) * used], pad], axis=0).astype(jnp.bfloat16)
        for b in range(per):
            out_ref[q * per + b] = part[:, b * LANES : (b + 1) * LANES]


def add_parts(parts):
    height, width = parts[0].shape
    used = height // QUARTERS
    return pl.pallas_call(
        functools.partial(gather_body, used),
        in_specs=[whole()] * len(parts),
        out_specs=whole(),
        out_shape=jax.ShapeDtypeStruct((QUARTERS * width // LANES, ROWS, LANES), jnp.bfloat16),
        compiler_params=pltpu.CompilerParams(vmem_limit_bytes=8 * MIB),
        name="add_parts",
    )(*parts)


def cos_turn(residue, npix, scale):
    residue = residue & (2 * npix - 1)
    x = (jnp.abs(residue - npix) - npix // 2).astype(jnp.float32) * scale
    square = x * x
    series = SINE[-1]
    for coefficient in SINE[-2::-1]:
        series = series * square + coefficient
    return series * x


def table_body(slots, npix_ref, mode_ref, noise_any, out_ref, noise_ref, coarse_ref, sems):
    chan_pos = lax.axis_index("chan")
    modes = mode_ref[...]
    modes = jnp.concatenate([modes, modes], axis=1)
    width = modes.shape[1]
    pixels = out_ref.shape[1]
    quarter = pixels // QUARTERS

    def noise_copy(j, q):
        cols = pl.ds(q * quarter, quarter)
        return pltpu.make_async_copy(noise_any.at[j, :, cols], noise_ref.at[j, :, cols], sems.at[j, q])

    for j in range(slots):
        for q in range(QUARTERS):

            @pl.when(q * quarter < npix_ref[chan_pos * slots + j])
            def _():
                noise_copy(j, q).start()

    weight = jnp.where(modes == 0, 1.0, 2.0).astype(jnp.float32) / math.sqrt(width)
    lane = lax.broadcasted_iota(jnp.int32, (1, width), 1)
    imag = jnp.where(lane >= width // 2, 1, 0)
    fine_row = lax.broadcasted_iota(jnp.int32, (FINE, width), 0)
    coarse_row = lax.broadcasted_iota(jnp.int32, (pixels // FINE, width), 0)
    per = quarter // FINE
    for j in range(slots):
        npix = npix_ref[chan_pos * slots + j]
        scale = jnp.float32(jnp.pi) / npix.astype(jnp.float32)
        turn = npix // 2
        fine = modes * (2 * fine_row + 1) + imag * turn
        same = cos_turn(fine, npix, scale) * weight
        cross = cos_turn(fine + turn, npix, scale) * weight
        coarse = modes * (2 * FINE * coarse_row)
        coarse_ref[0] = cos_turn(coarse, npix, scale)
        coarse_ref[1] = cos_turn(coarse + 3 * turn, npix, scale)

        def one_quarter(q, carry):
            for a in range(per):
                row = pl.ds(q * per + a, 1)
                values = coarse_ref[0, row, :] * same + coarse_ref[1, row, :] * cross
                start = pl.multiple_of(q * quarter + a * FINE, FINE)
                out_ref[j, pl.ds(start, FINE), :] = values.astype(jnp.bfloat16)
            return carry

        lax.fori_loop(0, npix // quarter, one_quarter, 0)

    for j in range(slots):
        for q in range(QUARTERS):

            @pl.when(q * quarter < npix_ref[chan_pos * slots + j])
            def _():
                noise_copy(j, q).wait()


def make_tables(npix, modes, inv_noise):
    slots, _, pixels = inv_noise.shape
    mode_count = modes.shape[1]
    return pl.pallas_call(
        functools.partial(table_body, slots),
        in_specs=[whole(pltpu.SMEM), whole(), whole(pl.ANY)],
        out_specs=[whole(), whole()],
        out_shape=[
            pltpu.VMEM((slots, pixels, 2 * mode_count), jnp.bfloat16),
            pltpu.VMEM(inv_noise.shape, jnp.bfloat16),
        ],
        scratch_shapes=[
            pltpu.VMEM((2, pixels // FINE, 2 * mode_count), jnp.float32),
            pltpu.SemaphoreType.DMA((slots, QUARTERS)),
        ],
        compiler_params=pltpu.CompilerParams(vmem_limit_bytes=16 * MIB),
        cost_estimate=pl.CostEstimate(
            flops=10 * slots * mode_count * pixels,
            bytes_accessed=4 * slots * mode_count * pixels,
            transcendentals=4 * slots * mode_count * LANES,
        ),
        name="make_tables",
    )(npix, modes, *in_hbm(inv_noise))


def middle_body(npix_ref, spec_ref, table_ref, noise_ref, out_ref, full_ref, turned_ref):
    mode_count = spec_ref.shape[0]
    slots, _, pixels = noise_ref.shape
    flat = mode_count * ROWS
    chan_pos = lax.axis_index("chan")
    full_ref[...] = spec_ref[...].reshape(flat, LANES).astype(jnp.float32)
    for s in range(slots):
        halves = [full_ref[pl.ds(2 * s + i, mode_count, stride=ROWS), :] for i in range(2)]
        turned_ref[s] = jnp.concatenate(halves, axis=0).T.astype(jnp.bfloat16)
    full_ref[...] = jnp.zeros((flat, LANES), jnp.float32)

    def one_channel(j, carry):
        spectra = turned_ref[j]
        npix = npix_ref[chan_pos * slots + j]
        for width in (pixels // 4, pixels // 2, pixels):

            @pl.when(npix == width)
            def _():
                table = table_ref[j, :width, :]
                sky = lax.dot_general(
                    spectra, table, (((1,), (1,)), ((), ())), preferred_element_type=jnp.float32
                )
                noisy = (noise_ref[j, :, :width].astype(jnp.float32) * sky).astype(jnp.bfloat16)
                back = jnp.dot(noisy, table, preferred_element_type=jnp.float32).T
                for i in range(2):
                    full_ref[pl.ds(2 * j + i, mode_count, stride=ROWS), :] = back[
                        i * mode_count : (i + 1) * mode_count
                    ]

        return carry

    lax.fori_loop(0, slots, one_channel, 0)
    out_ref[...] = full_ref[...].reshape(mode_count, ROWS, LANES).astype(jnp.bfloat16)


def middle(npix, spectra, tables, noise):
    slots, cycle_dev, _ = noise.shape
    mode_count = spectra.shape[0]
    return pl.pallas_call(
        middle_body,
        in_specs=[whole(pltpu.SMEM), whole(), whole(), whole()],
        out_specs=whole(),
        out_shape=jax.ShapeDtypeStruct(spectra.shape, jnp.bfloat16),
        scratch_shapes=[
            pltpu.VMEM((mode_count * ROWS, LANES), jnp.float32),
            pltpu.VMEM((slots, cycle_dev, 2 * mode_count), jnp.bfloat16),
        ],
        compiler_params=pltpu.CompilerParams(vmem_limit_bytes=20 * MIB),
        name="middle",
    )(npix, spectra, *in_vmem(tables, noise))


def backward_body(chans, slots, pixels, npix_ref, mix_ref, harm_ref, beam_ref, prior_ref, leg_ref, *rest):
    parts, out_ref, acc_ref = rest[:chans], rest[chans], rest[chans + 1]
    rows = [
        jnp.concatenate([part[b] for b in range(part.shape[0])], axis=1) for part in parts
    ]
    rows = jnp.concatenate(rows, axis=0)
    acc_ref[...] = lax.dot_general(
        leg_ref[0], rows, (((1,), (1,)), ((), ())), preferred_element_type=jnp.float32
    ).T
    chan_pos = lax.axis_index("chan")
    local_deg = beam_ref.shape[1]
    degrees = degrees_of((1, local_deg), chan_pos)
    comps = harm_ref.shape[0]
    totals = [prior_ref[k : k + 1, :] * harm_ref[k].astype(jnp.float32) for k in range(comps)]
    for s in range(chans):
        group = (chan_pos + chans - s) % chans
        for j in range(slots):
            c = group * slots + j
            filt = filter_row(beam_ref, npix_ref, c, degrees, local_deg * chans, pixels)
            weighted = acc_ref[pl.ds(s * ROWS + 2 * j, 2), :] * filt
            for k in range(comps):
                totals[k] = totals[k] + mix_ref[k, c] * weighted
    for k in range(comps):
        for i in range(2):
            out_ref[i, k] = totals[k][i : i + 1]


def backward(npix, mixing_t, harm, beam, prior, legendre, parts, slots, pixels):
    chans = len(parts)
    local_deg = legendre.shape[1]
    comps = harm.shape[0]
    return pl.pallas_call(
        functools.partial(backward_body, chans, slots, pixels),
        in_specs=[whole(pltpu.SMEM), whole(pltpu.SMEM)] + [whole()] * (4 + chans),
        out_specs=whole(),
        out_shape=jax.ShapeDtypeStruct((2, comps, 1, local_deg), jnp.float32),
        scratch_shapes=[pltpu.VMEM((chans * ROWS, local_deg), jnp.float32)],
        compiler_params=pltpu.CompilerParams(vmem_limit_bytes=16 * MIB),
        name="backward",
    )(npix, mixing_t, harm, beam, prior, legendre, *parts)


def on_device(
    harmonics, mixing, beam_window, prior_inv, legendre, inv_noise, mode_index, cycle_pixels
):
    chans = lax.axis_size("chan")
    slots, _, pixels = inv_noise.shape
    mixing_t = mixing.T
    harm = harmonics[:, :, 0, :].transpose(1, 0, 2)

    def shift(x, s):
        return lax.ppermute(x, "chan", [(d, (d + s) % chans) for d in range(chans)])

    parts = forward(
        cycle_pixels, mixing_t, harm, beam_window, legendre, chans, slots, pixels
    )
    parts = [parts[0]] + [shift(parts[s], s) for s in range(1, chans)]
    tables, noise = make_tables(cycle_pixels, mode_index[None, :], inv_noise)
    tables, noise, parts = lax.optimization_barrier((tables, noise, parts))
    chunks = add_parts(parts)
    spectra = lax.all_to_all(chunks, ("mset", "blk"), split_axis=0, concat_axis=0, tiled=True)
    returned = middle(cycle_pixels, spectra, tables, noise)
    own = lax.all_to_all(returned, ("mset", "blk"), split_axis=0, concat_axis=0, tiled=True)
    gathered = [own] + [shift(own, s) for s in range(1, chans)]
    return backward(
        cycle_pixels, mixing_t, harm, beam_window, prior_inv, legendre, gathered, slots, pixels
    )


def solution(mesh):
    placed = (
        P(None, None, ("mset", "blk"), "chan"),
        P(),
        P(None, "chan"),
        P(None, "chan"),
        P(("mset", "blk"), "chan", None),
        P("chan", ("mset", "blk"), None),
        P(),
        P(),
    )
    return jax.shard_map(
        on_device,
        mesh=mesh,
        in_specs=placed,
        out_specs=P(None, None, ("mset", "blk"), "chan"),
        check_vma=False,
    )
```

```python
import functools
import math

import jax
import jax.numpy as jnp
from jax import lax
from jax.experimental import pallas as pl
from jax.experimental.pallas import tpu as pltpu
from jax.sharding import PartitionSpec as P

MIB = 1 << 20
LANES = 128
ROWS = 8
QUARTERS = 4
STEPS = 4
FINE = 64
SINE = [(-1) ** n / math.factorial(2 * n + 1) for n in range(6)]


def whole(space=pltpu.VMEM):
    return pl.BlockSpec(memory_space=space)


def in_hbm(*arrays):
    return [pltpu.with_memory_space_constraint(x, pltpu.HBM) for x in arrays]


def in_vmem(*arrays):
    return [pltpu.with_memory_space_constraint(x, pltpu.VMEM) for x in arrays]


def filter_row(beam_ref, npix_ref, channel, degrees, total_deg, pixels):
    band_limit = total_deg * npix_ref[channel] // pixels - 1
    return jnp.where(degrees <= band_limit, beam_ref[pl.ds(channel, 1), :], 0.0)


def degrees_of(shape, chan_pos):
    return chan_pos * shape[-1] + lax.broadcasted_iota(jnp.int32, shape, len(shape) - 1)


def forward_body(chans, slots, pixels, npix_any, mix_any, harm_any, beam_any, prior_any, leg_any, *rest):
    outs = rest[:chans]
    base_ref, weight_ref, npix_ref, mix_ref, harm_ref, beam_ref, prior_ref = rest[chans : chans + 7]
    rows_ref, leg_ref, sems, small = rest[chans + 7 :]
    small_copies = [
        pltpu.make_async_copy(src, dst, small.at[n])
        for n, (src, dst) in enumerate(
            [
                (npix_any, npix_ref),
                (mix_any, mix_ref),
                (harm_any, harm_ref),
                (beam_any, beam_ref),
                (prior_any, prior_ref),
            ]
        )
    ]
    local_deg, cycles = leg_ref.shape
    block = cycles // STEPS
    per = STEPS // QUARTERS
    copies = [
        pltpu.make_async_copy(
            leg_any.at[0, :, pl.ds(q * block, block)],
            leg_ref.at[:, pl.ds(q * block, block)],
            sems.at[q],
        )
        for q in range(STEPS)
    ]
    for copy in small_copies + copies:
        copy.start()
    for copy in small_copies:
        copy.wait()
    chan_pos = lax.axis_index("chan")
    degrees = degrees_of((1, local_deg), chan_pos)
    comps = [harm_ref[k].astype(jnp.float32) for k in range(harm_ref.shape[0])]
    for s in range(chans):
        group = (chan_pos + s) % chans
        for j in range(slots):
            c = group * slots + j
            mixture = sum(mix_ref[k, c] * comps[k] for k in range(len(comps)))
            filt = filter_row(beam_ref, npix_ref, c, degrees, local_deg * chans, pixels)
            rows_ref[pl.ds(s * ROWS + 2 * j, 2), :] = mixture * filt
            for k in range(len(comps)):
                row = ((chans - s) % chans * slots + j) * len(comps) + k
                weight_ref[pl.ds(row, 1), :] = mix_ref[k, c] * filt
        rest_rows = ROWS - 2 * slots
        rows_ref[pl.ds(s * ROWS + 2 * slots, rest_rows), :] = jnp.zeros(
            (rest_rows, local_deg), jnp.float32
        )
    for k in range(len(comps)):
        base_ref[pl.ds(2 * k, 2), :] = prior_ref[k : k + 1, :] * comps[k]
    rows = rows_ref[...].astype(jnp.bfloat16)
    used = 2 * slots
    for q in range(STEPS):
        copies[q].wait()
        partial = jnp.dot(
            rows, leg_ref[:, q * block : (q + 1) * block], preferred_element_type=jnp.float32
        )
        for s in range(chans):
            outs[s][pl.ds(q // per * used, used), pl.ds(q % per * block, block)] = partial[
                s * ROWS : s * ROWS + used
            ].astype(jnp.bfloat16)


def forward(npix, mixing_t, harm, beam, prior, legendre, chans, slots, pixels):
    _, local_deg, cycles = legendre.shape
    comps = harm.shape[0]
    used = 2 * slots
    return pl.pallas_call(
        functools.partial(forward_body, chans, slots, pixels),
        in_specs=[whole(pl.ANY)] * 6,
        out_specs=[whole()] * (chans + 2),
        out_shape=[jax.ShapeDtypeStruct((QUARTERS * used, cycles // QUARTERS), jnp.bfloat16)] * chans
        + [
            jax.ShapeDtypeStruct((2 * comps, local_deg), jnp.float32),
            jax.ShapeDtypeStruct((chans * slots * comps, local_deg), jnp.float32),
        ],
        scratch_shapes=[
            pltpu.SMEM(npix.shape, npix.dtype),
            pltpu.SMEM(mixing_t.shape, mixing_t.dtype),
            pltpu.VMEM(harm.shape, harm.dtype),
            pltpu.VMEM(beam.shape, beam.dtype),
            pltpu.VMEM(prior.shape, prior.dtype),
            pltpu.VMEM((chans * ROWS, local_deg), jnp.float32),
            pltpu.VMEM((local_deg, cycles), jnp.bfloat16),
            pltpu.SemaphoreType.DMA((STEPS,)),
            pltpu.SemaphoreType.DMA((5,)),
        ],
        compiler_params=pltpu.CompilerParams(vmem_limit_bytes=16 * MIB),
        cost_estimate=pl.CostEstimate(
            flops=2 * chans * ROWS * local_deg * cycles,
            bytes_accessed=2 * local_deg * cycles,
            transcendentals=0,
        ),
        name="forward",
    )(*in_hbm(npix, mixing_t, harm, beam, prior, legendre))


def gather_body(used, *refs):
    out_ref = refs[-1]
    total = refs[0][...].astype(jnp.float32)
    for ref in refs[1:-1]:
        total = total + ref[...].astype(jnp.float32)
    width = total.shape[1]
    per = width // LANES
    pad = jnp.zeros((ROWS - used, width), jnp.float32)
    for q in range(total.shape[0] // used):
        part = jnp.concatenate([total[q * used : (q + 1) * used], pad], axis=0).astype(jnp.bfloat16)
        for b in range(per):
            out_ref[q * per + b] = part[:, b * LANES : (b + 1) * LANES]


def add_parts(parts):
    height, width = parts[0].shape
    used = height // QUARTERS
    return pl.pallas_call(
        functools.partial(gather_body, used),
        in_specs=[whole()] * len(parts),
        out_specs=whole(),
        out_shape=jax.ShapeDtypeStruct((QUARTERS * width // LANES, ROWS, LANES), jnp.bfloat16),
        compiler_params=pltpu.CompilerParams(vmem_limit_bytes=8 * MIB),
        name="add_parts",
    )(*parts)


def cos_turn(residue, npix, scale):
    residue = residue & (2 * npix - 1)
    x = (jnp.abs(residue - npix) - npix // 2).astype(jnp.float32) * scale
    square = x * x
    series = SINE[-1]
    for coefficient in SINE[-2::-1]:
        series = series * square + coefficient
    return series * x


def table_body(npix_ref, mode_ref, noise_any, out_ref, noise_ref, coarse_ref, sems):
    slots = out_ref.shape[0]
    chan_pos = lax.axis_index("chan")
    modes = mode_ref[...]
    modes = jnp.concatenate([modes, modes], axis=1)
    width = modes.shape[1]
    pixels = out_ref.shape[1]
    quarter = pixels // QUARTERS

    def noise_copy(j, q):
        cols = pl.ds(q * quarter, quarter)
        return pltpu.make_async_copy(noise_any.at[j, :, cols], noise_ref.at[j, :, cols], sems.at[j, q])

    for j in range(slots):
        for q in range(QUARTERS):

            @pl.when(q * quarter < npix_ref[chan_pos * slots + j])
            def _():
                noise_copy(j, q).start()

    weight = jnp.where(modes == 0, 1.0, 2.0).astype(jnp.float32) / math.sqrt(width)
    lane = lax.broadcasted_iota(jnp.int32, (1, width), 1)
    imag = jnp.where(lane >= width // 2, 1, 0)
    fine_row = lax.broadcasted_iota(jnp.int32, (FINE, width), 0)
    coarse_row = lax.broadcasted_iota(jnp.int32, (pixels // FINE, width), 0)
    per = quarter // FINE
    for j in range(slots):
        npix = npix_ref[chan_pos * slots + j]
        scale = jnp.float32(jnp.pi) / npix.astype(jnp.float32)
        turn = npix // 2
        fine = modes * (2 * fine_row + 1) + imag * turn
        same = cos_turn(fine, npix, scale) * weight
        cross = cos_turn(fine + turn, npix, scale) * weight
        coarse = modes * (2 * FINE * coarse_row)
        coarse_ref[0] = cos_turn(coarse, npix, scale)
        coarse_ref[1] = cos_turn(coarse + 3 * turn, npix, scale)

        def one_quarter(q, carry):
            for a in range(per):
                row = pl.ds(q * per + a, 1)
                values = coarse_ref[0, row, :] * same + coarse_ref[1, row, :] * cross
                start = pl.multiple_of(q * quarter + a * FINE, FINE)
                out_ref[j, pl.ds(start, FINE), :] = values.astype(jnp.bfloat16)
            return carry

        lax.fori_loop(0, npix // quarter, one_quarter, 0)

    for j in range(slots):
        for q in range(QUARTERS):

            @pl.when(q * quarter < npix_ref[chan_pos * slots + j])
            def _():
                noise_copy(j, q).wait()


def make_tables(npix, modes, inv_noise):
    slots, _, pixels = inv_noise.shape
    mode_count = modes.shape[1]
    return pl.pallas_call(
        table_body,
        in_specs=[whole(pltpu.SMEM), whole(), whole(pl.ANY)],
        out_specs=[whole()] * 2,
        out_shape=[
            pltpu.VMEM((slots, pixels, 2 * mode_count), jnp.bfloat16),
            pltpu.VMEM(inv_noise.shape, jnp.bfloat16),
        ],
        scratch_shapes=[
            pltpu.VMEM((2, pixels // FINE, 2 * mode_count), jnp.float32),
            pltpu.SemaphoreType.DMA((slots, QUARTERS)),
        ],
        compiler_params=pltpu.CompilerParams(vmem_limit_bytes=16 * MIB),
        cost_estimate=pl.CostEstimate(
            flops=10 * slots * mode_count * pixels,
            bytes_accessed=4 * slots * mode_count * pixels,
            transcendentals=4 * slots * mode_count * LANES,
        ),
        name="make_tables",
    )(npix, modes, *in_hbm(inv_noise))


def middle_body(npix_ref, spec_ref, table_ref, noise_ref, out_ref, full_ref, turned_ref):
    mode_count = spec_ref.shape[0]
    slots, _, pixels = noise_ref.shape
    flat = mode_count * ROWS
    chan_pos = lax.axis_index("chan")
    full_ref[...] = spec_ref[...].reshape(flat, LANES).astype(jnp.float32)
    for s in range(slots):
        halves = [full_ref[pl.ds(2 * s + i, mode_count, stride=ROWS), :] for i in range(2)]
        turned_ref[s] = jnp.concatenate(halves, axis=0).T.astype(jnp.bfloat16)
    full_ref[...] = jnp.zeros((flat, LANES), jnp.float32)

    def one_channel(j, carry):
        spectra = turned_ref[j]
        npix = npix_ref[chan_pos * slots + j]
        for width in (pixels // 4, pixels // 2, pixels):

            @pl.when(npix == width)
            def _():
                table = table_ref[j, :width, :]
                sky = lax.dot_general(
                    spectra, table, (((1,), (1,)), ((), ())), preferred_element_type=jnp.float32
                )
                noisy = (noise_ref[j, :, :width].astype(jnp.float32) * sky).astype(jnp.bfloat16)
                back = jnp.dot(noisy, table, preferred_element_type=jnp.float32).T
                for i in range(2):
                    full_ref[pl.ds(2 * j + i, mode_count, stride=ROWS), :] = back[
                        i * mode_count : (i + 1) * mode_count
                    ]

        return carry

    lax.fori_loop(0, slots, one_channel, 0)
    out_ref[...] = full_ref[...].reshape(mode_count, ROWS, LANES).astype(jnp.bfloat16)


def middle(npix, spectra, tables, noise):
    slots, cycle_dev, _ = noise.shape
    mode_count = spectra.shape[0]
    return pl.pallas_call(
        middle_body,
        in_specs=[whole(pltpu.SMEM), whole(), whole(), whole()],
        out_specs=whole(),
        out_shape=jax.ShapeDtypeStruct(spectra.shape, jnp.bfloat16),
        scratch_shapes=[
            pltpu.VMEM((mode_count * ROWS, LANES), jnp.float32),
            pltpu.VMEM((slots, cycle_dev, 2 * mode_count), jnp.bfloat16),
        ],
        compiler_params=pltpu.CompilerParams(vmem_limit_bytes=20 * MIB),
        name="middle",
    )(npix, spectra, *in_vmem(tables, noise))


def pack_body(used, chunk_ref, out_ref):
    per = out_ref.shape[1] // LANES
    for q in range(QUARTERS):
        tiles = [chunk_ref[q * per + b] for b in range(per)]
        rows = jnp.concatenate(tiles, axis=1).astype(jnp.float32)
        out_ref[pl.ds(q * used, used), :] = rows[:used].astype(jnp.bfloat16)


def pack(chunks, used):
    blocks = chunks.shape[0]
    return pl.pallas_call(
        functools.partial(pack_body, used),
        in_specs=[whole()],
        out_specs=whole(),
        out_shape=jax.ShapeDtypeStruct((QUARTERS * used, blocks // QUARTERS * LANES), chunks.dtype),
        compiler_params=pltpu.CompilerParams(vmem_limit_bytes=8 * MIB),
        name="pack",
    )(chunks)


def backward_body(base_ref, weight_ref, leg_ref, *rest):
    parts, out_ref, acc_ref = rest[:-2], rest[-2], rest[-1]
    height, block = parts[0].shape
    used = height // QUARTERS
    comps = base_ref.shape[0] // 2
    rows = jnp.concatenate([part[...] for part in parts], axis=0)
    owner = lax.broadcasted_iota(jnp.int32, rows.shape, 0) % height // used
    total = None
    for q in range(QUARTERS):
        mine = jnp.where(owner == q, rows.astype(jnp.float32), 0.0).astype(jnp.bfloat16)
        product = lax.dot_general(
            leg_ref[0, :, q * block : (q + 1) * block],
            mine,
            (((1,), (1,)), ((), ())),
            preferred_element_type=jnp.float32,
        )
        total = product if q == 0 else total + product
    acc_ref[...] = total.T
    sums = [base_ref[pl.ds(2 * k, 2), :] for k in range(comps)]
    for s in range(len(parts)):
        for j in range(used // 2):
            value = sum(acc_ref[pl.ds(s * height + q * used + 2 * j, 2), :] for q in range(QUARTERS))
            for k in range(comps):
                row = (s * (used // 2) + j) * comps + k
                sums[k] = sums[k] + weight_ref[pl.ds(row, 1), :] * value
    for k in range(comps):
        for i in range(2):
            out_ref[i, k] = sums[k][i : i + 1]


def backward(base, weights, legendre, parts):
    local_deg = legendre.shape[1]
    return pl.pallas_call(
        backward_body,
        in_specs=[whole()] * (3 + len(parts)),
        out_specs=whole(),
        out_shape=jax.ShapeDtypeStruct((2, base.shape[0] // 2, 1, local_deg), jnp.float32),
        scratch_shapes=[pltpu.VMEM((len(parts) * parts[0].shape[0], local_deg), jnp.float32)],
        compiler_params=pltpu.CompilerParams(vmem_limit_bytes=16 * MIB),
        name="backward",
    )(base, weights, legendre, *parts)


def on_device(
    harmonics, mixing, beam_window, prior_inv, legendre, inv_noise, mode_index, cycle_pixels
):
    chans = lax.axis_size("chan")
    slots, _, pixels = inv_noise.shape
    mixing_t = mixing.T
    harm = harmonics[:, :, 0, :].transpose(1, 0, 2)

    def shift(x, s):
        return lax.ppermute(x, "chan", [(d, (d + s) % chans) for d in range(chans)])

    *parts, base, weights = forward(
        cycle_pixels, mixing_t, harm, beam_window, prior_inv, legendre, chans, slots, pixels
    )
    parts = [parts[0]] + [shift(parts[s], s) for s in range(1, chans)]
    tables, noise = make_tables(cycle_pixels, mode_index[None, :], inv_noise)
    tables, noise, parts = lax.optimization_barrier((tables, noise, parts))
    chunks = add_parts(parts)
    spectra = lax.all_to_all(chunks, ("mset", "blk"), split_axis=0, concat_axis=0, tiled=True)
    returned = middle(cycle_pixels, spectra, tables, noise)
    own = lax.all_to_all(returned, ("mset", "blk"), split_axis=0, concat_axis=0, tiled=True)
    own = pack(own, 2 * slots)
    gathered = [own] + [shift(own, s) for s in range(1, chans)]
    return backward(base, weights, legendre, gathered)


def solution(mesh):
    placed = (
        P(None, None, ("mset", "blk"), "chan"),
        P(),
        P(None, "chan"),
        P(None, "chan"),
        P(("mset", "blk"), "chan", None),
        P("chan", ("mset", "blk"), None),
        P(),
        P(),
    )
    return jax.shard_map(
        on_device,
        mesh=mesh,
        in_specs=placed,
        out_specs=P(None, None, ("mset", "blk"), "chan"),
        check_vma=False,
    )
```

```python
import functools
import math

import jax
import jax.numpy as jnp
from jax import lax
from jax.experimental import pallas as pl
from jax.experimental.pallas import tpu as pltpu
from jax.sharding import PartitionSpec as P

MIB = 1 << 20
LANES = 128
ROWS = 8
QUARTERS = 4
STEPS = 8
FINE = 64
SINE = [(-1) ** n / math.factorial(2 * n + 1) for n in range(6)]


def whole(space=pltpu.VMEM):
    return pl.BlockSpec(memory_space=space)


def in_hbm(*arrays):
    return [pltpu.with_memory_space_constraint(x, pltpu.HBM) for x in arrays]


def in_vmem(*arrays):
    return [pltpu.with_memory_space_constraint(x, pltpu.VMEM) for x in arrays]


def filter_row(beam_ref, npix_ref, channel, degrees, total_deg, pixels):
    band_limit = total_deg * npix_ref[channel] // pixels - 1
    return jnp.where(degrees <= band_limit, beam_ref[pl.ds(channel, 1), :], 0.0)


def degrees_of(shape, chan_pos):
    return chan_pos * shape[-1] + lax.broadcasted_iota(jnp.int32, shape, len(shape) - 1)


def forward_body(chans, slots, pixels, npix_any, mix_any, harm_any, beam_any, prior_any, leg_any, *rest):
    outs = rest[:chans]
    base_ref, weight_ref, npix_ref, mix_ref, harm_ref, beam_ref, prior_ref = rest[chans : chans + 7]
    rows_ref, leg_ref, sems, small = rest[chans + 7 :]
    small_copies = [
        pltpu.make_async_copy(src, dst, small.at[n])
        for n, (src, dst) in enumerate(
            [
                (npix_any, npix_ref),
                (mix_any, mix_ref),
                (harm_any, harm_ref),
                (beam_any, beam_ref),
                (prior_any, prior_ref),
            ]
        )
    ]
    local_deg, cycles = leg_ref.shape
    block = cycles // STEPS
    per = STEPS // QUARTERS
    copies = [
        pltpu.make_async_copy(
            leg_any.at[0, :, pl.ds(q * block, block)],
            leg_ref.at[:, pl.ds(q * block, block)],
            sems.at[q],
        )
        for q in range(STEPS)
    ]
    for copy in small_copies:
        copy.start()
    for copy in copies:
        copy.start(priority=1)
    for copy in small_copies:
        copy.wait()
    chan_pos = lax.axis_index("chan")
    degrees = degrees_of((1, local_deg), chan_pos)
    comps = [harm_ref[k].astype(jnp.float32) for k in range(harm_ref.shape[0])]
    for s in range(chans):
        group = (chan_pos + s) % chans
        for j in range(slots):
            c = group * slots + j
            mixture = sum(mix_ref[k, c] * comps[k] for k in range(len(comps)))
            filt = filter_row(beam_ref, npix_ref, c, degrees, local_deg * chans, pixels)
            rows_ref[pl.ds(s * ROWS + 2 * j, 2), :] = mixture * filt
            for k in range(len(comps)):
                row = ((chans - s) % chans * slots + j) * len(comps) + k
                weight_ref[pl.ds(row, 1), :] = mix_ref[k, c] * filt
        rest_rows = ROWS - 2 * slots
        rows_ref[pl.ds(s * ROWS + 2 * slots, rest_rows), :] = jnp.zeros(
            (rest_rows, local_deg), jnp.float32
        )
    for k in range(len(comps)):
        base_ref[pl.ds(2 * k, 2), :] = prior_ref[k : k + 1, :] * comps[k]
    rows = rows_ref[...].astype(jnp.bfloat16)
    used = 2 * slots
    for q in range(STEPS):
        copies[q].wait()
        partial = jnp.dot(
            rows, leg_ref[:, q * block : (q + 1) * block], preferred_element_type=jnp.float32
        )
        for s in range(chans):
            outs[s][pl.ds(q // per * used, used), pl.ds(q % per * block, block)] = partial[
                s * ROWS : s * ROWS + used
            ].astype(jnp.bfloat16)


def forward(npix, mixing_t, harm, beam, prior, legendre, chans, slots, pixels):
    _, local_deg, cycles = legendre.shape
    comps = harm.shape[0]
    used = 2 * slots
    return pl.pallas_call(
        functools.partial(forward_body, chans, slots, pixels),
        in_specs=[whole(pl.ANY)] * 6,
        out_specs=[whole()] * (chans + 2),
        out_shape=[jax.ShapeDtypeStruct((QUARTERS * used, cycles // QUARTERS), jnp.bfloat16)] * chans
        + [
            jax.ShapeDtypeStruct((2 * comps, local_deg), jnp.float32),
            jax.ShapeDtypeStruct((chans * slots * comps, local_deg), jnp.float32),
        ],
        scratch_shapes=[
            pltpu.SMEM(npix.shape, npix.dtype),
            pltpu.SMEM(mixing_t.shape, mixing_t.dtype),
            pltpu.VMEM(harm.shape, harm.dtype),
            pltpu.VMEM(beam.shape, beam.dtype),
            pltpu.VMEM(prior.shape, prior.dtype),
            pltpu.VMEM((chans * ROWS, local_deg), jnp.float32),
            pltpu.VMEM((local_deg, cycles), jnp.bfloat16),
            pltpu.SemaphoreType.DMA((STEPS,)),
            pltpu.SemaphoreType.DMA((5,)),
        ],
        compiler_params=pltpu.CompilerParams(vmem_limit_bytes=16 * MIB),
        cost_estimate=pl.CostEstimate(
            flops=2 * chans * ROWS * local_deg * cycles,
            bytes_accessed=2 * local_deg * cycles,
            transcendentals=0,
        ),
        name="forward",
    )(*in_hbm(npix, mixing_t, harm, beam, prior, legendre))


def gather_body(used, *refs):
    out_ref = refs[-1]
    total = refs[0][...].astype(jnp.float32)
    for ref in refs[1:-1]:
        total = total + ref[...].astype(jnp.float32)
    width = total.shape[1]
    per = width // LANES
    pad = jnp.zeros((ROWS - used, width), jnp.float32)
    for q in range(total.shape[0] // used):
        part = jnp.concatenate([total[q * used : (q + 1) * used], pad], axis=0).astype(jnp.bfloat16)
        for b in range(per):
            out_ref[q * per + b] = part[:, b * LANES : (b + 1) * LANES]


def add_parts(parts):
    height, width = parts[0].shape
    used = height // QUARTERS
    return pl.pallas_call(
        functools.partial(gather_body, used),
        in_specs=[whole()] * len(parts),
        out_specs=whole(),
        out_shape=jax.ShapeDtypeStruct((QUARTERS * width // LANES, ROWS, LANES), jnp.bfloat16),
        compiler_params=pltpu.CompilerParams(vmem_limit_bytes=8 * MIB),
        name="add_parts",
    )(*parts)


def cos_turn(residue, npix, scale):
    residue = residue & (2 * npix - 1)
    x = (jnp.abs(residue - npix) - npix // 2).astype(jnp.float32) * scale
    square = x * x
    series = SINE[-1]
    for coefficient in SINE[-2::-1]:
        series = series * square + coefficient
    return series * x


def table_body(npix_ref, mode_ref, noise_any, out_ref, noise_ref, coarse_ref, sems):
    slots = out_ref.shape[0]
    chan_pos = lax.axis_index("chan")
    modes = mode_ref[...]
    modes = jnp.concatenate([modes, modes], axis=1)
    width = modes.shape[1]
    pixels = out_ref.shape[1]
    quarter = pixels // QUARTERS

    def noise_copy(j, q):
        cols = pl.ds(q * quarter, quarter)
        return pltpu.make_async_copy(noise_any.at[j, :, cols], noise_ref.at[j, :, cols], sems.at[j, q])

    for j in range(slots):
        for q in range(QUARTERS):

            @pl.when(q * quarter < npix_ref[chan_pos * slots + j])
            def _():
                noise_copy(j, q).start()

    weight = jnp.where(modes == 0, 1.0, 2.0).astype(jnp.float32) / math.sqrt(width)
    lane = lax.broadcasted_iota(jnp.int32, (1, width), 1)
    imag = jnp.where(lane >= width // 2, 1, 0)
    fine_row = lax.broadcasted_iota(jnp.int32, (FINE, width), 0)
    coarse_row = lax.broadcasted_iota(jnp.int32, (pixels // FINE, width), 0)
    per = quarter // FINE
    for j in range(slots):
        npix = npix_ref[chan_pos * slots + j]
        scale = jnp.float32(jnp.pi) / npix.astype(jnp.float32)
        turn = npix // 2
        fine = modes * (2 * fine_row + 1) + imag * turn
        same = cos_turn(fine, npix, scale) * weight
        cross = cos_turn(fine + turn, npix, scale) * weight
        coarse = modes * (2 * FINE * coarse_row)
        coarse_ref[0] = cos_turn(coarse, npix, scale)
        coarse_ref[1] = cos_turn(coarse + 3 * turn, npix, scale)

        def one_quarter(q, carry):
            for a in range(per):
                row = pl.ds(q * per + a, 1)
                values = coarse_ref[0, row, :] * same + coarse_ref[1, row, :] * cross
                start = pl.multiple_of(q * quarter + a * FINE, FINE)
                out_ref[j, pl.ds(start, FINE), :] = values.astype(jnp.bfloat16)
            return carry

        lax.fori_loop(0, npix // quarter, one_quarter, 0)

    for j in range(slots):
        for q in range(QUARTERS):

            @pl.when(q * quarter < npix_ref[chan_pos * slots + j])
            def _():
                noise_copy(j, q).wait()


def make_tables(npix, modes, inv_noise):
    slots, _, pixels = inv_noise.shape
    mode_count = modes.shape[1]
    return pl.pallas_call(
        table_body,
        in_specs=[whole(pltpu.SMEM), whole(), whole(pl.ANY)],
        out_specs=[whole()] * 2,
        out_shape=[
            pltpu.VMEM((slots, pixels, 2 * mode_count), jnp.bfloat16),
            pltpu.VMEM(inv_noise.shape, jnp.bfloat16),
        ],
        scratch_shapes=[
            pltpu.VMEM((2, pixels // FINE, 2 * mode_count), jnp.float32),
            pltpu.SemaphoreType.DMA((slots, QUARTERS)),
        ],
        compiler_params=pltpu.CompilerParams(vmem_limit_bytes=16 * MIB),
        cost_estimate=pl.CostEstimate(
            flops=10 * slots * mode_count * pixels,
            bytes_accessed=4 * slots * mode_count * pixels,
            transcendentals=4 * slots * mode_count * LANES,
        ),
        name="make_tables",
    )(npix, modes, *in_hbm(inv_noise))


def middle_body(npix_ref, spec_ref, table_ref, noise_ref, out_ref, full_ref, turned_ref):
    mode_count = spec_ref.shape[0]
    slots, _, pixels = noise_ref.shape
    flat = mode_count * ROWS
    chan_pos = lax.axis_index("chan")
    full_ref[...] = spec_ref[...].reshape(flat, LANES).astype(jnp.float32)
    for s in range(slots):
        halves = [full_ref[pl.ds(2 * s + i, mode_count, stride=ROWS), :] for i in range(2)]
        turned_ref[s] = jnp.concatenate(halves, axis=0).T.astype(jnp.bfloat16)
    full_ref[...] = jnp.zeros((flat, LANES), jnp.float32)

    def one_channel(j, carry):
        spectra = turned_ref[j]
        npix = npix_ref[chan_pos * slots + j]
        for width in (pixels // 4, pixels // 2, pixels):

            @pl.when(npix == width)
            def _():
                table = table_ref[j, :width, :]
                sky = lax.dot_general(
                    spectra, table, (((1,), (1,)), ((), ())), preferred_element_type=jnp.float32
                )
                noisy = (noise_ref[j, :, :width].astype(jnp.float32) * sky).astype(jnp.bfloat16)
                back = jnp.dot(noisy, table, preferred_element_type=jnp.float32).T
                for i in range(2):
                    full_ref[pl.ds(2 * j + i, mode_count, stride=ROWS), :] = back[
                        i * mode_count : (i + 1) * mode_count
                    ]

        return carry

    lax.fori_loop(0, slots, one_channel, 0)
    out_ref[...] = full_ref[...].reshape(mode_count, ROWS, LANES).astype(jnp.bfloat16)


def middle(npix, spectra, tables, noise):
    slots, cycle_dev, _ = noise.shape
    mode_count = spectra.shape[0]
    return pl.pallas_call(
        middle_body,
        in_specs=[whole(pltpu.SMEM), whole(), whole(), whole()],
        out_specs=whole(),
        out_shape=jax.ShapeDtypeStruct(spectra.shape, jnp.bfloat16),
        scratch_shapes=[
            pltpu.VMEM((mode_count * ROWS, LANES), jnp.float32),
            pltpu.VMEM((slots, cycle_dev, 2 * mode_count), jnp.bfloat16),
        ],
        compiler_params=pltpu.CompilerParams(vmem_limit_bytes=20 * MIB),
        name="middle",
    )(npix, spectra, *in_vmem(tables, noise))


def pack_body(used, chunk_ref, out_ref):
    per = out_ref.shape[1] // LANES
    for q in range(QUARTERS):
        tiles = [chunk_ref[q * per + b] for b in range(per)]
        rows = jnp.concatenate(tiles, axis=1).astype(jnp.float32)
        out_ref[pl.ds(q * used, used), :] = rows[:used].astype(jnp.bfloat16)


def pack(chunks, used):
    blocks = chunks.shape[0]
    return pl.pallas_call(
        functools.partial(pack_body, used),
        in_specs=[whole()],
        out_specs=whole(),
        out_shape=jax.ShapeDtypeStruct((QUARTERS * used, blocks // QUARTERS * LANES), chunks.dtype),
        compiler_params=pltpu.CompilerParams(vmem_limit_bytes=8 * MIB),
        name="pack",
    )(chunks)


def backward_body(base_ref, weight_ref, leg_ref, *rest):
    parts, out_ref, acc_ref = rest[:-2], rest[-2], rest[-1]
    height, block = parts[0].shape
    used = height // QUARTERS
    comps = base_ref.shape[0] // 2
    rows = jnp.concatenate([part[...] for part in parts], axis=0)
    local_deg = leg_ref.shape[1]
    owner = lax.broadcasted_iota(jnp.int32, (local_deg, rows.shape[0]), 1) % height // used
    total = None
    for q in range(QUARTERS):
        product = lax.dot_general(
            leg_ref[0, :, q * block : (q + 1) * block],
            rows,
            (((1,), (1,)), ((), ())),
            preferred_element_type=jnp.float32,
        )
        total = product if q == 0 else jnp.where(owner == q, product, total)
    acc_ref[...] = total.T
    sums = [base_ref[pl.ds(2 * k, 2), :] for k in range(comps)]
    for s in range(len(parts)):
        for j in range(used // 2):
            value = sum(acc_ref[pl.ds(s * height + q * used + 2 * j, 2), :] for q in range(QUARTERS))
            for k in range(comps):
                row = (s * (used // 2) + j) * comps + k
                sums[k] = sums[k] + weight_ref[pl.ds(row, 1), :] * value
    for k in range(comps):
        for i in range(2):
            out_ref[i, k] = sums[k][i : i + 1]


def backward(base, weights, legendre, parts):
    local_deg = legendre.shape[1]
    return pl.pallas_call(
        backward_body,
        in_specs=[whole()] * (3 + len(parts)),
        out_specs=whole(),
        out_shape=jax.ShapeDtypeStruct((2, base.shape[0] // 2, 1, local_deg), jnp.float32),
        scratch_shapes=[pltpu.VMEM((len(parts) * parts[0].shape[0], local_deg), jnp.float32)],
        compiler_params=pltpu.CompilerParams(vmem_limit_bytes=16 * MIB),
        name="backward",
    )(base, weights, legendre, *parts)


def on_device(
    harmonics, mixing, beam_window, prior_inv, legendre, inv_noise, mode_index, cycle_pixels
):
    chans = lax.axis_size("chan")
    slots, _, pixels = inv_noise.shape
    mixing_t = mixing.T
    harm = harmonics[:, :, 0, :].transpose(1, 0, 2)

    def shift(x, s):
        return lax.ppermute(x, "chan", [(d, (d + s) % chans) for d in range(chans)])

    *parts, base, weights = forward(
        cycle_pixels, mixing_t, harm, beam_window, prior_inv, legendre, chans, slots, pixels
    )
    parts = [parts[0]] + [shift(parts[s], s) for s in range(1, chans)]
    tables, noise = make_tables(cycle_pixels, mode_index[None, :], inv_noise)
    tables, noise, parts = lax.optimization_barrier((tables, noise, parts))
    chunks = add_parts(parts)
    spectra = lax.all_to_all(chunks, ("mset", "blk"), split_axis=0, concat_axis=0, tiled=True)
    returned = middle(cycle_pixels, spectra, tables, noise)
    own = lax.all_to_all(returned, ("mset", "blk"), split_axis=0, concat_axis=0, tiled=True)
    own = pack(own, 2 * slots)
    gathered = [own] + [shift(own, s) for s in range(1, chans)]
    return backward(base, weights, legendre, gathered)


def solution(mesh):
    placed = (
        P(None, None, ("mset", "blk"), "chan"),
        P(),
        P(None, "chan"),
        P(None, "chan"),
        P(("mset", "blk"), "chan", None),
        P("chan", ("mset", "blk"), None),
        P(),
        P(),
    )
    return jax.shard_map(
        on_device,
        mesh=mesh,
        in_specs=placed,
        out_specs=P(None, None, ("mset", "blk"), "chan"),
        check_vma=False,
    )
```

```python
import functools
import math

import jax
import jax.numpy as jnp
from jax import lax
from jax.experimental import pallas as pl
from jax.experimental.pallas import tpu as pltpu
from jax.sharding import PartitionSpec as P

MIB = 1 << 20
LANES = 128
ROWS = 8
QUARTERS = 4
STEPS = 8
FINE = 64
SINE = [(-1) ** n / math.factorial(2 * n + 1) for n in range(6)]


def whole(space=pltpu.VMEM):
    return pl.BlockSpec(memory_space=space)


def in_hbm(*arrays):
    return [pltpu.with_memory_space_constraint(x, pltpu.HBM) for x in arrays]


def in_vmem(*arrays):
    return [pltpu.with_memory_space_constraint(x, pltpu.VMEM) for x in arrays]


def filter_row(beam_ref, npix_ref, channel, degrees, total_deg, pixels):
    band_limit = total_deg * npix_ref[channel] // pixels - 1
    return jnp.where(degrees <= band_limit, beam_ref[pl.ds(channel, 1), :], 0.0)


def degrees_of(shape, chan_pos):
    return chan_pos * shape[-1] + lax.broadcasted_iota(jnp.int32, shape, len(shape) - 1)


def forward_body(chans, slots, pixels, npix_any, mix_any, harm_any, beam_any, prior_any, leg_any, *rest):
    outs = rest[:chans]
    base_ref, weight_ref, npix_ref, mix_ref, harm_ref, beam_ref, prior_ref = rest[chans : chans + 7]
    rows_ref, leg_ref, sems, small = rest[chans + 7 :]
    small_copies = [
        pltpu.make_async_copy(src, dst, small.at[n])
        for n, (src, dst) in enumerate(
            [
                (npix_any, npix_ref),
                (mix_any, mix_ref),
                (harm_any, harm_ref),
                (beam_any, beam_ref),
                (prior_any, prior_ref),
            ]
        )
    ]
    local_deg, cycles = leg_ref.shape
    block = cycles // STEPS
    per = STEPS // QUARTERS
    copies = [
        pltpu.make_async_copy(
            leg_any.at[0, :, pl.ds(q * block, block)],
            leg_ref.at[:, pl.ds(q * block, block)],
            sems.at[q],
        )
        for q in range(STEPS)
    ]
    for copy in small_copies:
        copy.start()
    for copy in copies:
        copy.start(priority=1)
    for copy in small_copies:
        copy.wait()
    chan_pos = lax.axis_index("chan")
    degrees = degrees_of((1, local_deg), chan_pos)
    comps = [harm_ref[k].astype(jnp.float32) for k in range(harm_ref.shape[0])]
    for s in range(chans):
        group = (chan_pos + s) % chans
        for j in range(slots):
            c = group * slots + j
            mixture = sum(mix_ref[k, c] * comps[k] for k in range(len(comps)))
            filt = filter_row(beam_ref, npix_ref, c, degrees, local_deg * chans, pixels)
            rows_ref[pl.ds(s * ROWS + 2 * j, 2), :] = mixture * filt
            for k in range(len(comps)):
                row = ((chans - s) % chans * slots + j) * len(comps) + k
                weight_ref[pl.ds(row, 1), :] = mix_ref[k, c] * filt
        rest_rows = ROWS - 2 * slots
        rows_ref[pl.ds(s * ROWS + 2 * slots, rest_rows), :] = jnp.zeros(
            (rest_rows, local_deg), jnp.float32
        )
    for k in range(len(comps)):
        base_ref[pl.ds(2 * k, 2), :] = prior_ref[k : k + 1, :] * comps[k]
    rows = rows_ref[...].astype(jnp.bfloat16)
    used = 2 * slots
    for q in range(STEPS):
        copies[q].wait()
        partial = jnp.dot(
            rows, leg_ref[:, q * block : (q + 1) * block], preferred_element_type=jnp.float32
        )
        for s in range(chans):
            outs[s][pl.ds(q // per * used, used), pl.ds(q % per * block, block)] = partial[
                s * ROWS : s * ROWS + used
            ].astype(jnp.bfloat16)


def forward(npix, mixing_t, harm, beam, prior, legendre, chans, slots, pixels):
    _, local_deg, cycles = legendre.shape
    comps = harm.shape[0]
    used = 2 * slots
    return pl.pallas_call(
        functools.partial(forward_body, chans, slots, pixels),
        in_specs=[whole(pl.ANY)] * 6,
        out_specs=[whole()] * (chans + 2),
        out_shape=[jax.ShapeDtypeStruct((QUARTERS * used, cycles // QUARTERS), jnp.bfloat16)] * chans
        + [
            jax.ShapeDtypeStruct((2 * comps, local_deg), jnp.float32),
            jax.ShapeDtypeStruct((chans * slots * comps, local_deg), jnp.float32),
        ],
        scratch_shapes=[
            pltpu.SMEM(npix.shape, npix.dtype),
            pltpu.SMEM(mixing_t.shape, mixing_t.dtype),
            pltpu.VMEM(harm.shape, harm.dtype),
            pltpu.VMEM(beam.shape, beam.dtype),
            pltpu.VMEM(prior.shape, prior.dtype),
            pltpu.VMEM((chans * ROWS, local_deg), jnp.float32),
            pltpu.VMEM((local_deg, cycles), jnp.bfloat16),
            pltpu.SemaphoreType.DMA((STEPS,)),
            pltpu.SemaphoreType.DMA((5,)),
        ],
        compiler_params=pltpu.CompilerParams(vmem_limit_bytes=16 * MIB),
        cost_estimate=pl.CostEstimate(
            flops=2 * chans * ROWS * local_deg * cycles,
            bytes_accessed=2 * local_deg * cycles,
            transcendentals=0,
        ),
        name="forward",
    )(*in_hbm(npix, mixing_t, harm, beam, prior, legendre))


def gather_body(used, *refs):
    out_ref = refs[-1]
    total = refs[0][...].astype(jnp.float32)
    for ref in refs[1:-1]:
        total = total + ref[...].astype(jnp.float32)
    width = total.shape[1]
    per = width // LANES
    pad = jnp.zeros((ROWS - used, width), jnp.float32)
    for q in range(total.shape[0] // used):
        part = jnp.concatenate([total[q * used : (q + 1) * used], pad], axis=0).astype(jnp.bfloat16)
        for b in range(per):
            out_ref[q * per + b] = part[:, b * LANES : (b + 1) * LANES]


def add_parts(parts):
    height, width = parts[0].shape
    used = height // QUARTERS
    return pl.pallas_call(
        functools.partial(gather_body, used),
        in_specs=[whole()] * len(parts),
        out_specs=whole(),
        out_shape=jax.ShapeDtypeStruct((QUARTERS * width // LANES, ROWS, LANES), jnp.bfloat16),
        compiler_params=pltpu.CompilerParams(vmem_limit_bytes=8 * MIB),
        name="add_parts",
    )(*parts)


def cos_turn(residue, npix, scale):
    residue = residue & (2 * npix - 1)
    x = (jnp.abs(residue - npix) - npix // 2).astype(jnp.float32) * scale
    square = x * x
    series = SINE[-1]
    for coefficient in SINE[-2::-1]:
        series = series * square + coefficient
    return series * x


def table_body(npix_ref, mode_ref, noise_any, out_ref, noise_ref, coarse_ref, sems):
    slots = out_ref.shape[0]
    chan_pos = lax.axis_index("chan")
    modes = mode_ref[...]
    modes = jnp.concatenate([modes, modes], axis=1)
    width = modes.shape[1]
    pixels = out_ref.shape[1]
    quarter = pixels // QUARTERS

    def noise_copy(j, q):
        cols = pl.ds(q * quarter, quarter)
        return pltpu.make_async_copy(noise_any.at[j, :, cols], noise_ref.at[j, :, cols], sems.at[j, q])

    for j in range(slots):
        for q in range(QUARTERS):

            @pl.when(q * quarter < npix_ref[chan_pos * slots + j])
            def _():
                noise_copy(j, q).start()

    weight = jnp.where(modes == 0, 1.0, 2.0).astype(jnp.float32) / math.sqrt(width)
    lane = lax.broadcasted_iota(jnp.int32, (1, width), 1)
    imag = jnp.where(lane >= width // 2, 1, 0)
    fine_row = lax.broadcasted_iota(jnp.int32, (FINE, width), 0)
    coarse_row = lax.broadcasted_iota(jnp.int32, (pixels // FINE, width), 0)
    per = quarter // FINE
    for j in range(slots):
        npix = npix_ref[chan_pos * slots + j]
        scale = jnp.float32(jnp.pi) / npix.astype(jnp.float32)
        turn = npix // 2
        fine = modes * (2 * fine_row + 1) + imag * turn
        same = cos_turn(fine, npix, scale) * weight
        cross = cos_turn(fine + turn, npix, scale) * weight
        coarse = modes * (2 * FINE * coarse_row)
        coarse_ref[0] = cos_turn(coarse, npix, scale)
        coarse_ref[1] = cos_turn(coarse + 3 * turn, npix, scale)

        def one_quarter(q, carry):
            for a in range(per):
                row = pl.ds(q * per + a, 1)
                values = coarse_ref[0, row, :] * same + coarse_ref[1, row, :] * cross
                start = pl.multiple_of(q * quarter + a * FINE, FINE)
                out_ref[j, pl.ds(start, FINE), :] = values.astype(jnp.bfloat16)
            return carry

        lax.fori_loop(0, npix // quarter, one_quarter, 0)

    for j in range(slots):
        for q in range(QUARTERS):

            @pl.when(q * quarter < npix_ref[chan_pos * slots + j])
            def _():
                noise_copy(j, q).wait()


def make_tables(npix, modes, inv_noise):
    slots, _, pixels = inv_noise.shape
    mode_count = modes.shape[1]
    return pl.pallas_call(
        table_body,
        in_specs=[whole(pltpu.SMEM), whole(), whole(pl.ANY)],
        out_specs=[whole()] * 2,
        out_shape=[
            pltpu.VMEM((slots, pixels, 2 * mode_count), jnp.bfloat16),
            pltpu.VMEM(inv_noise.shape, jnp.bfloat16),
        ],
        scratch_shapes=[
            pltpu.VMEM((2, pixels // FINE, 2 * mode_count), jnp.float32),
            pltpu.SemaphoreType.DMA((slots, QUARTERS)),
        ],
        compiler_params=pltpu.CompilerParams(vmem_limit_bytes=16 * MIB),
        cost_estimate=pl.CostEstimate(
            flops=10 * slots * mode_count * pixels,
            bytes_accessed=4 * slots * mode_count * pixels,
            transcendentals=4 * slots * mode_count * LANES,
        ),
        name="make_tables",
    )(npix, modes, *in_hbm(inv_noise))


def middle_body(npix_ref, spec_ref, table_ref, noise_ref, out_ref, full_ref, turned_ref):
    mode_count = spec_ref.shape[0]
    slots, _, pixels = noise_ref.shape
    flat = mode_count * ROWS
    chan_pos = lax.axis_index("chan")
    full_ref[...] = spec_ref[...].reshape(flat, LANES).astype(jnp.float32)
    for s in range(slots):
        halves = [full_ref[pl.ds(2 * s + i, mode_count, stride=ROWS), :] for i in range(2)]
        turned_ref[s] = jnp.concatenate(halves, axis=0).T.astype(jnp.bfloat16)

    def one_channel(j, carry):
        spectra = turned_ref[j]
        npix = npix_ref[chan_pos * slots + j]
        for width in (pixels // 4, pixels // 2, pixels):

            @pl.when(npix == width)
            def _():
                table = table_ref[j, :width, :]
                sky = lax.dot_general(
                    spectra, table, (((1,), (1,)), ((), ())), preferred_element_type=jnp.float32
                )
                noisy = (noise_ref[j, :, :width].astype(jnp.float32) * sky).astype(jnp.bfloat16)
                back = jnp.dot(noisy, table, preferred_element_type=jnp.float32).T
                for i in range(2):
                    full_ref[pl.ds(2 * j + i, mode_count, stride=ROWS), :] = back[
                        i * mode_count : (i + 1) * mode_count
                    ]

        return carry

    lax.fori_loop(0, slots, one_channel, 0)
    out_ref[...] = full_ref[...].reshape(mode_count, ROWS, LANES).astype(jnp.bfloat16)


def middle(npix, spectra, tables, noise):
    slots, cycle_dev, _ = noise.shape
    mode_count = spectra.shape[0]
    return pl.pallas_call(
        middle_body,
        in_specs=[whole(pltpu.SMEM), whole(), whole(), whole()],
        out_specs=whole(),
        out_shape=jax.ShapeDtypeStruct(spectra.shape, jnp.bfloat16),
        scratch_shapes=[
            pltpu.VMEM((mode_count * ROWS, LANES), jnp.float32),
            pltpu.VMEM((slots, cycle_dev, 2 * mode_count), jnp.bfloat16),
        ],
        compiler_params=pltpu.CompilerParams(vmem_limit_bytes=20 * MIB),
        name="middle",
    )(npix, spectra, *in_vmem(tables, noise))


def pack_body(used, chunk_ref, out_ref):
    per = out_ref.shape[1] // LANES
    for q in range(QUARTERS):
        tiles = [chunk_ref[q * per + b] for b in range(per)]
        rows = jnp.concatenate(tiles, axis=1).astype(jnp.float32)
        out_ref[pl.ds(q * used, used), :] = rows[:used].astype(jnp.bfloat16)


def pack(chunks, used):
    blocks = chunks.shape[0]
    return pl.pallas_call(
        functools.partial(pack_body, used),
        in_specs=[whole()],
        out_specs=whole(),
        out_shape=jax.ShapeDtypeStruct((QUARTERS * used, blocks // QUARTERS * LANES), chunks.dtype),
        compiler_params=pltpu.CompilerParams(vmem_limit_bytes=8 * MIB),
        name="pack",
    )(chunks)


def backward_body(base_ref, weight_ref, leg_ref, *rest):
    parts, out_ref, acc_ref = rest[:-2], rest[-2], rest[-1]
    height, block = parts[0].shape
    used = height // QUARTERS
    comps = base_ref.shape[0] // 2
    rows = jnp.concatenate([part[...] for part in parts], axis=0)
    local_deg = leg_ref.shape[1]
    owner = lax.broadcasted_iota(jnp.int32, (local_deg, rows.shape[0]), 1) % height // used
    total = None
    for q in range(QUARTERS):
        product = lax.dot_general(
            leg_ref[0, :, q * block : (q + 1) * block],
            rows,
            (((1,), (1,)), ((), ())),
            preferred_element_type=jnp.float32,
        )
        total = product if q == 0 else jnp.where(owner == q, product, total)
    acc_ref[...] = total.T
    sums = [base_ref[pl.ds(2 * k, 2), :] for k in range(comps)]
    for s in range(len(parts)):
        for j in range(used // 2):
            value = sum(acc_ref[pl.ds(s * height + q * used + 2 * j, 2), :] for q in range(QUARTERS))
            for k in range(comps):
                row = (s * (used // 2) + j) * comps + k
                sums[k] = sums[k] + weight_ref[pl.ds(row, 1), :] * value
    for k in range(comps):
        for i in range(2):
            out_ref[i, k] = sums[k][i : i + 1]


def backward(base, weights, legendre, parts):
    local_deg = legendre.shape[1]
    return pl.pallas_call(
        backward_body,
        in_specs=[whole()] * (3 + len(parts)),
        out_specs=whole(),
        out_shape=jax.ShapeDtypeStruct((2, base.shape[0] // 2, 1, local_deg), jnp.float32),
        scratch_shapes=[pltpu.VMEM((len(parts) * parts[0].shape[0], local_deg), jnp.float32)],
        compiler_params=pltpu.CompilerParams(vmem_limit_bytes=16 * MIB),
        name="backward",
    )(base, weights, legendre, *parts)


def on_device(
    harmonics, mixing, beam_window, prior_inv, legendre, inv_noise, mode_index, cycle_pixels
):
    chans = lax.axis_size("chan")
    slots, _, pixels = inv_noise.shape
    mixing_t = mixing.T
    harm = harmonics[:, :, 0, :].transpose(1, 0, 2)

    def shift(x, s):
        return lax.ppermute(x, "chan", [(d, (d + s) % chans) for d in range(chans)])

    *parts, base, weights = forward(
        cycle_pixels, mixing_t, harm, beam_window, prior_inv, legendre, chans, slots, pixels
    )
    parts = [parts[0]] + [shift(parts[s], s) for s in (1, chans - 1, *range(2, chans - 1))]
    tables, noise = make_tables(cycle_pixels, mode_index[None, :], inv_noise)
    tables, noise, parts = lax.optimization_barrier((tables, noise, parts))
    chunks = add_parts(parts)
    spectra = lax.all_to_all(chunks, ("mset", "blk"), split_axis=0, concat_axis=0, tiled=True)
    returned = middle(cycle_pixels, spectra, tables, noise)
    own = lax.all_to_all(returned, ("mset", "blk"), split_axis=0, concat_axis=0, tiled=True)
    own = pack(own, 2 * slots)
    gathered = [own] + [shift(own, s) for s in range(1, chans)]
    return backward(base, weights, legendre, gathered)


def solution(mesh):
    placed = (
        P(None, None, ("mset", "blk"), "chan"),
        P(),
        P(None, "chan"),
        P(None, "chan"),
        P(("mset", "blk"), "chan", None),
        P("chan", ("mset", "blk"), None),
        P(),
        P(),
    )
    return jax.shard_map(
        on_device,
        mesh=mesh,
        in_specs=placed,
        out_specs=P(None, None, ("mset", "blk"), "chan"),
        check_vma=False,
    )
```

```python
import functools
import math

import jax
import jax.numpy as jnp
from jax import lax
from jax.experimental import pallas as pl
from jax.experimental.pallas import tpu as pltpu
from jax.sharding import PartitionSpec as P

MIB = 1 << 20
LANES = 128
ROWS = 8
QUARTERS = 4
STEPS = 8
FINE = 64
SINE = [(-1) ** n / math.factorial(2 * n + 1) for n in range(6)]


def whole(space=pltpu.VMEM):
    return pl.BlockSpec(memory_space=space)


def in_hbm(*arrays):
    return [pltpu.with_memory_space_constraint(x, pltpu.HBM) for x in arrays]


def in_vmem(*arrays):
    return [pltpu.with_memory_space_constraint(x, pltpu.VMEM) for x in arrays]


def filter_row(beam_ref, npix_ref, channel, degrees, total_deg, pixels):
    band_limit = total_deg * npix_ref[channel] // pixels - 1
    return jnp.where(degrees <= band_limit, beam_ref[pl.ds(channel, 1), :], 0.0)


def last_order(chans):
    return [0, 1, chans - 1, *range(2, chans - 1)]


def degrees_of(shape, chan_pos):
    return chan_pos * shape[-1] + lax.broadcasted_iota(jnp.int32, shape, len(shape) - 1)


def forward_body(chans, slots, pixels, npix_any, mix_any, harm_any, beam_any, prior_any, leg_any, *rest):
    outs = rest[:chans]
    base_ref, weight_ref, npix_ref, mix_ref, harm_ref, beam_ref, prior_ref = rest[chans : chans + 7]
    rows_ref, leg_ref, sems, small = rest[chans + 7 :]
    small_copies = [
        pltpu.make_async_copy(src, dst, small.at[n])
        for n, (src, dst) in enumerate(
            [
                (npix_any, npix_ref),
                (mix_any, mix_ref),
                (harm_any, harm_ref),
                (beam_any, beam_ref),
                (prior_any, prior_ref),
            ]
        )
    ]
    local_deg, cycles = leg_ref.shape
    block = cycles // STEPS
    per = STEPS // QUARTERS
    copies = [
        pltpu.make_async_copy(
            leg_any.at[0, :, pl.ds(q * block, block)],
            leg_ref.at[:, pl.ds(q * block, block)],
            sems.at[q],
        )
        for q in range(STEPS)
    ]
    for copy in small_copies:
        copy.start()
    for copy in copies:
        copy.start(priority=1)
    for copy in small_copies:
        copy.wait()
    chan_pos = lax.axis_index("chan")
    degrees = degrees_of((1, local_deg), chan_pos)
    comps = [harm_ref[k].astype(jnp.float32) for k in range(harm_ref.shape[0])]
    for s in range(chans):
        group = (chan_pos + s) % chans
        for j in range(slots):
            c = group * slots + j
            mixture = sum(mix_ref[k, c] * comps[k] for k in range(len(comps)))
            filt = filter_row(beam_ref, npix_ref, c, degrees, local_deg * chans, pixels)
            rows_ref[pl.ds(s * ROWS + 2 * j, 2), :] = mixture * filt
            for k in range(len(comps)):
                place = last_order(chans).index((chans - s) % chans)
                row = (place * slots + j) * len(comps) + k
                weight_ref[pl.ds(row, 1), :] = mix_ref[k, c] * filt
        rest_rows = ROWS - 2 * slots
        rows_ref[pl.ds(s * ROWS + 2 * slots, rest_rows), :] = jnp.zeros(
            (rest_rows, local_deg), jnp.float32
        )
    for k in range(len(comps)):
        base_ref[pl.ds(2 * k, 2), :] = prior_ref[k : k + 1, :] * comps[k]
    rows = rows_ref[...].astype(jnp.bfloat16)
    used = 2 * slots
    for q in range(STEPS):
        copies[q].wait()
        partial = jnp.dot(
            rows, leg_ref[:, q * block : (q + 1) * block], preferred_element_type=jnp.float32
        )
        for s in range(chans):
            outs[s][pl.ds(q // per * used, used), pl.ds(q % per * block, block)] = partial[
                s * ROWS : s * ROWS + used
            ].astype(jnp.bfloat16)


def forward(npix, mixing_t, harm, beam, prior, legendre, chans, slots, pixels):
    _, local_deg, cycles = legendre.shape
    comps = harm.shape[0]
    used = 2 * slots
    return pl.pallas_call(
        functools.partial(forward_body, chans, slots, pixels),
        in_specs=[whole(pl.ANY)] * 6,
        out_specs=[whole()] * (chans + 2),
        out_shape=[jax.ShapeDtypeStruct((QUARTERS * used, cycles // QUARTERS), jnp.bfloat16)] * chans
        + [
            jax.ShapeDtypeStruct((2 * comps, local_deg), jnp.float32),
            jax.ShapeDtypeStruct((chans * slots * comps, local_deg), jnp.float32),
        ],
        scratch_shapes=[
            pltpu.SMEM(npix.shape, npix.dtype),
            pltpu.SMEM(mixing_t.shape, mixing_t.dtype),
            pltpu.VMEM(harm.shape, harm.dtype),
            pltpu.VMEM(beam.shape, beam.dtype),
            pltpu.VMEM(prior.shape, prior.dtype),
            pltpu.VMEM((chans * ROWS, local_deg), jnp.float32),
            pltpu.VMEM((local_deg, cycles), jnp.bfloat16),
            pltpu.SemaphoreType.DMA((STEPS,)),
            pltpu.SemaphoreType.DMA((5,)),
        ],
        compiler_params=pltpu.CompilerParams(vmem_limit_bytes=16 * MIB),
        cost_estimate=pl.CostEstimate(
            flops=2 * chans * ROWS * local_deg * cycles,
            bytes_accessed=2 * local_deg * cycles,
            transcendentals=0,
        ),
        name="forward",
    )(*in_hbm(npix, mixing_t, harm, beam, prior, legendre))


def gather_body(used, *refs):
    out_ref = refs[-1]
    total = refs[0][...].astype(jnp.float32)
    for ref in refs[1:-1]:
        total = total + ref[...].astype(jnp.float32)
    width = total.shape[1]
    per = width // LANES
    pad = jnp.zeros((ROWS - used, width), jnp.float32)
    for q in range(total.shape[0] // used):
        part = jnp.concatenate([total[q * used : (q + 1) * used], pad], axis=0).astype(jnp.bfloat16)
        for b in range(per):
            out_ref[q * per + b] = part[:, b * LANES : (b + 1) * LANES]


def add_parts(parts):
    height, width = parts[0].shape
    used = height // QUARTERS
    return pl.pallas_call(
        functools.partial(gather_body, used),
        in_specs=[whole()] * len(parts),
        out_specs=whole(),
        out_shape=jax.ShapeDtypeStruct((QUARTERS * width // LANES, ROWS, LANES), jnp.bfloat16),
        compiler_params=pltpu.CompilerParams(vmem_limit_bytes=8 * MIB),
        name="add_parts",
    )(*parts)


def cos_turn(residue, npix, scale):
    residue = residue & (2 * npix - 1)
    x = (jnp.abs(residue - npix) - npix // 2).astype(jnp.float32) * scale
    square = x * x
    series = SINE[-1]
    for coefficient in SINE[-2::-1]:
        series = series * square + coefficient
    return series * x


def table_body(npix_ref, mode_ref, noise_any, out_ref, noise_ref, coarse_ref, sems):
    slots = out_ref.shape[0]
    chan_pos = lax.axis_index("chan")
    modes = mode_ref[...]
    modes = jnp.concatenate([modes, modes], axis=1)
    width = modes.shape[1]
    pixels = out_ref.shape[1]
    quarter = pixels // QUARTERS

    def noise_copy(j, q):
        cols = pl.ds(q * quarter, quarter)
        return pltpu.make_async_copy(noise_any.at[j, :, cols], noise_ref.at[j, :, cols], sems.at[j, q])

    for j in range(slots):
        for q in range(QUARTERS):

            @pl.when(q * quarter < npix_ref[chan_pos * slots + j])
            def _():
                noise_copy(j, q).start()

    weight = jnp.where(modes == 0, 1.0, 2.0).astype(jnp.float32) / math.sqrt(width)
    lane = lax.broadcasted_iota(jnp.int32, (1, width), 1)
    imag = jnp.where(lane >= width // 2, 1, 0)
    fine_row = lax.broadcasted_iota(jnp.int32, (FINE, width), 0)
    coarse_row = lax.broadcasted_iota(jnp.int32, (pixels // FINE, width), 0)
    per = quarter // FINE
    for j in range(slots):
        npix = npix_ref[chan_pos * slots + j]
        scale = jnp.float32(jnp.pi) / npix.astype(jnp.float32)
        turn = npix // 2
        fine = modes * (2 * fine_row + 1) + imag * turn
        same = cos_turn(fine, npix, scale) * weight
        cross = cos_turn(fine + turn, npix, scale) * weight
        coarse = modes * (2 * FINE * coarse_row)
        coarse_ref[0] = cos_turn(coarse, npix, scale)
        coarse_ref[1] = cos_turn(coarse + 3 * turn, npix, scale)

        def one_quarter(q, carry):
            for a in range(per):
                row = pl.ds(q * per + a, 1)
                values = coarse_ref[0, row, :] * same + coarse_ref[1, row, :] * cross
                start = pl.multiple_of(q * quarter + a * FINE, FINE)
                out_ref[j, pl.ds(start, FINE), :] = values.astype(jnp.bfloat16)
            return carry

        lax.fori_loop(0, npix // quarter, one_quarter, 0)

    for j in range(slots):
        for q in range(QUARTERS):

            @pl.when(q * quarter < npix_ref[chan_pos * slots + j])
            def _():
                noise_copy(j, q).wait()


def make_tables(npix, modes, inv_noise):
    slots, _, pixels = inv_noise.shape
    mode_count = modes.shape[1]
    return pl.pallas_call(
        table_body,
        in_specs=[whole(pltpu.SMEM), whole(), whole(pl.ANY)],
        out_specs=[whole()] * 2,
        out_shape=[
            pltpu.VMEM((slots, pixels, 2 * mode_count), jnp.bfloat16),
            pltpu.VMEM(inv_noise.shape, jnp.bfloat16),
        ],
        scratch_shapes=[
            pltpu.VMEM((2, pixels // FINE, 2 * mode_count), jnp.float32),
            pltpu.SemaphoreType.DMA((slots, QUARTERS)),
        ],
        compiler_params=pltpu.CompilerParams(vmem_limit_bytes=16 * MIB),
        cost_estimate=pl.CostEstimate(
            flops=10 * slots * mode_count * pixels,
            bytes_accessed=4 * slots * mode_count * pixels,
            transcendentals=4 * slots * mode_count * LANES,
        ),
        name="make_tables",
    )(npix, modes, *in_hbm(inv_noise))


def middle_body(npix_any, spec_ref, table_ref, noise_ref, out_ref, full_ref, turned_ref, npix_ref, sem):
    copy = pltpu.make_async_copy(npix_any, npix_ref, sem)
    copy.start()
    mode_count = spec_ref.shape[0]
    slots, _, pixels = noise_ref.shape
    flat = mode_count * ROWS
    chan_pos = lax.axis_index("chan")
    full_ref[...] = spec_ref[...].reshape(flat, LANES).astype(jnp.float32)
    for s in range(slots):
        halves = [full_ref[pl.ds(2 * s + i, mode_count, stride=ROWS), :] for i in range(2)]
        turned_ref[s] = jnp.concatenate(halves, axis=0).T.astype(jnp.bfloat16)

    copy.wait()

    def one_channel(j, carry):
        spectra = turned_ref[j]
        npix = npix_ref[chan_pos * slots + j]
        for width in (pixels // 4, pixels // 2, pixels):

            @pl.when(npix == width)
            def _():
                table = table_ref[j, :width, :]
                sky = lax.dot_general(
                    spectra, table, (((1,), (1,)), ((), ())), preferred_element_type=jnp.float32
                )
                noisy = (noise_ref[j, :, :width].astype(jnp.float32) * sky).astype(jnp.bfloat16)
                back = jnp.dot(noisy, table, preferred_element_type=jnp.float32).T
                for i in range(2):
                    full_ref[pl.ds(2 * j + i, mode_count, stride=ROWS), :] = back[
                        i * mode_count : (i + 1) * mode_count
                    ]

        return carry

    lax.fori_loop(0, slots, one_channel, 0)
    out_ref[...] = full_ref[...].reshape(mode_count, ROWS, LANES).astype(jnp.bfloat16)


def middle(npix, spectra, tables, noise):
    slots, cycle_dev, _ = noise.shape
    mode_count = spectra.shape[0]
    return pl.pallas_call(
        middle_body,
        in_specs=[whole(pl.ANY), whole(), whole(), whole()],
        out_specs=whole(),
        out_shape=jax.ShapeDtypeStruct(spectra.shape, jnp.bfloat16),
        scratch_shapes=[
            pltpu.VMEM((mode_count * ROWS, LANES), jnp.float32),
            pltpu.VMEM((slots, cycle_dev, 2 * mode_count), jnp.bfloat16),
            pltpu.SMEM(npix.shape, npix.dtype),
            pltpu.SemaphoreType.DMA,
        ],
        compiler_params=pltpu.CompilerParams(vmem_limit_bytes=20 * MIB),
        name="middle",
    )(npix, spectra, *in_vmem(tables, noise))


def pack_body(used, chunk_ref, out_ref):
    per = out_ref.shape[1] // LANES
    for q in range(QUARTERS):
        tiles = [chunk_ref[q * per + b] for b in range(per)]
        rows = jnp.concatenate(tiles, axis=1).astype(jnp.float32)
        out_ref[pl.ds(q * used, used), :] = rows[:used].astype(jnp.bfloat16)


def pack(chunks, used):
    blocks = chunks.shape[0]
    return pl.pallas_call(
        functools.partial(pack_body, used),
        in_specs=[whole()],
        out_specs=whole(),
        out_shape=jax.ShapeDtypeStruct((QUARTERS * used, blocks // QUARTERS * LANES), chunks.dtype),
        compiler_params=pltpu.CompilerParams(vmem_limit_bytes=8 * MIB),
        name="pack",
    )(chunks)


def backward_body(base_ref, weight_ref, leg_ref, *rest):
    parts, out_ref, acc_ref = rest[:-2], rest[-2], rest[-1]
    height, block = parts[0].shape
    used = height // QUARTERS
    comps = base_ref.shape[0] // 2
    rows = jnp.concatenate([part[...] for part in parts], axis=0)
    local_deg = leg_ref.shape[1]
    owner = lax.broadcasted_iota(jnp.int32, (local_deg, rows.shape[0]), 1) % height // used
    total = None
    for q in range(QUARTERS):
        product = lax.dot_general(
            leg_ref[0, :, q * block : (q + 1) * block],
            rows,
            (((1,), (1,)), ((), ())),
            preferred_element_type=jnp.float32,
        )
        total = product if q == 0 else jnp.where(owner == q, product, total)
    acc_ref[...] = total.T
    sums = [base_ref[pl.ds(2 * k, 2), :] for k in range(comps)]
    for s in range(len(parts)):
        for j in range(used // 2):
            value = sum(acc_ref[pl.ds(s * height + q * used + 2 * j, 2), :] for q in range(QUARTERS))
            for k in range(comps):
                row = (s * (used // 2) + j) * comps + k
                sums[k] = sums[k] + weight_ref[pl.ds(row, 1), :] * value
    for k in range(comps):
        for i in range(2):
            out_ref[i, k] = sums[k][i : i + 1]


def backward(base, weights, legendre, parts):
    local_deg = legendre.shape[1]
    return pl.pallas_call(
        backward_body,
        in_specs=[whole()] * (3 + len(parts)),
        out_specs=whole(),
        out_shape=jax.ShapeDtypeStruct((2, base.shape[0] // 2, 1, local_deg), jnp.float32),
        scratch_shapes=[pltpu.VMEM((len(parts) * parts[0].shape[0], local_deg), jnp.float32)],
        compiler_params=pltpu.CompilerParams(vmem_limit_bytes=16 * MIB),
        name="backward",
    )(base, weights, legendre, *parts)


def on_device(
    harmonics, mixing, beam_window, prior_inv, legendre, inv_noise, mode_index, cycle_pixels
):
    chans = lax.axis_size("chan")
    slots, _, pixels = inv_noise.shape
    mixing_t = mixing.T
    harm = harmonics[:, :, 0, :].transpose(1, 0, 2)

    def shift(x, s):
        return lax.ppermute(x, "chan", [(d, (d + s) % chans) for d in range(chans)])

    *parts, base, weights = forward(
        cycle_pixels, mixing_t, harm, beam_window, prior_inv, legendre, chans, slots, pixels
    )
    parts = [parts[0]] + [shift(parts[s], s) for s in (1, chans - 1, *range(2, chans - 1))]
    tables, noise = make_tables(cycle_pixels, mode_index[None, :], inv_noise)
    tables, noise, parts = lax.optimization_barrier((tables, noise, parts))
    chunks = add_parts(parts)
    spectra = lax.all_to_all(chunks, ("mset", "blk"), split_axis=0, concat_axis=0, tiled=True)
    returned = middle(cycle_pixels, spectra, tables, noise)
    own = lax.all_to_all(returned, ("mset", "blk"), split_axis=0, concat_axis=0, tiled=True)
    own = pack(own, 2 * slots)
    gathered = [own] + [shift(own, s) for s in last_order(chans)[1:]]
    return backward(base, weights, legendre, gathered)


def solution(mesh):
    placed = (
        P(None, None, ("mset", "blk"), "chan"),
        P(),
        P(None, "chan"),
        P(None, "chan"),
        P(("mset", "blk"), "chan", None),
        P("chan", ("mset", "blk"), None),
        P(),
        P(),
    )
    return jax.shard_map(
        on_device,
        mesh=mesh,
        in_specs=placed,
        out_specs=P(None, None, ("mset", "blk"), "chan"),
        check_vma=False,
    )
```
